32 devices in a mesh: lat: 8 (over z, core), lon: 4 (over y, x).
Axes of the slice: x: 2, y: 2, z: 4, core: 2. Of those that a mesh axis runs over, the one named last changes fastest.
Arguments:
- latent: float32 [64, 112, 640], P('lat', 'lon'), may hold values from -6 to 6
- conv_first: float32 [25, 640], replicated, may hold values from -1.2 to 1.2
- conv_second: float32 [25, 640], replicated, may hold values from -1.2 to 1.2
- filter_gains: float32 [48, 640], P(None, 'lon'), may hold values from -4 to 4
- norm_gain: float32 [640], replicated, may hold values from 0.5 to 1.5
- up_weight: bfloat16 [640, 1280], replicated, may hold values from -0.25 to 0.25
- down_weight: bfloat16 [1280, 640], replicated, may hold values from -0.15625 to 0.15625
Outputs:
- block_out: float32 [64, 112, 640], P('lat', 'lon')
The draws below stay inside these ranges and needn't reach their ends.
All inputs are finite; a program needn't handle non-finite values.
Results may differ from the reference program's by a relative error of at most 0.0012.
Values sent between devices are 32-bit elements; how exact they have to be, the bound alone decides.
A program may use at most 64 MiB of HBM per device.

```python
import jax
import jax.numpy as jnp
from jax import lax

C = 640
HIDDEN_SIZE = 1280
MODES = 48
NLAT = 64
NLON = 112


def steps_of(key, shape, pieces, low, top_value):
    def one(axis_at, blocks):
        steps = jax.random.uniform(jax.random.fold_in(jax.random.fold_in(key, 6), axis_at), (blocks,), jnp.float32, low / len(pieces), top_value / len(pieces))
        return jnp.repeat(jnp.exp(steps), shape[axis_at] // blocks).reshape((-1,) + (1,) * (len(shape) - axis_at - 1))

    gain = one(*pieces[0])
    for cut in pieces[1:]:
        gain = gain * one(*cut)
    return gain


def bell_draw(stream_key, dims, deviation, bound, pieces=(), kind=jnp.bfloat16):
    gain = steps_of(stream_key, dims, pieces, -0.22, 0.18) if pieces else 1.0
    values = jax.random.normal(stream_key, dims, jnp.float32) * deviation * gain
    return jnp.minimum(jnp.maximum(values, -bound), bound).astype(kind)


def setup_inputs(seed: int = 0) -> dict:
    key_of = jax.random.split(jax.random.key(seed), 8)
    return {
        "latent": bell_draw(key_of[0], (NLAT, NLON, C), 1.0, 6.0, ((0, 8), (1, 4)), jnp.float32),
        "conv_first": bell_draw(key_of[1], (25, C), 0.2, 1.2, (), jnp.float32),
        "conv_second": bell_draw(key_of[2], (25, C), 0.2, 1.2, (), jnp.float32),
        "filter_gains": bell_draw(key_of[3], (MODES, C), 1.0, 4.0, ((1, 4),), jnp.float32),
        "norm_gain": jnp.clip(1.0 + 0.1 * jax.random.normal(key_of[4], (C,), jnp.float32), 0.5, 1.5),
        "up_weight": bell_draw(key_of[5], (C, HIDDEN_SIZE), C ** -0.5, 0.25),
        "down_weight": bell_draw(key_of[6], (HIDDEN_SIZE, C), HIDDEN_SIZE ** -0.5, 0.15625),
    }


highest = lax.Precision.HIGHEST

def stencil_sum(padded, weights, row_count, col_count):
    stencil_total = jnp.zeros((row_count, col_count, padded.shape[2]), padded.dtype)
    for row_shift in range(5):
        for col_shift in range(5):
            stencil_total = stencil_total + weights[row_shift * 5 + col_shift] * padded[row_shift:row_shift + row_count, col_shift:col_shift + col_count, :]
    return stencil_total

def local_stencil(latent, weights):
    wrapped = jnp.concatenate([latent[:, -2:], latent, latent[:, :2]], axis=1)
    padded = jnp.pad(wrapped, ((2, 2), (0, 0), (0, 0)))
    return stencil_sum(padded, weights, latent.shape[0], latent.shape[1])

def colatitude(cell_count, float_type):
    cell_index = jnp.arange(cell_count).astype(jnp.int32).astype(float_type)
    return jnp.pi * (cell_index + 0.5) / cell_count

def legendre_table(orders, degrees, cosine, sine_theta):
    log_seed = 0.5 * (jnp.log((2.0 * orders + 1.0) / (4.0 * jnp.pi)) + jax.scipy.special.gammaln(2.0 * orders + 1.0) - 2.0 * orders * jnp.log(2.0) - 2.0 * jax.scipy.special.gammaln(orders + 1.0))
    diagonal_term = jnp.exp(log_seed[:, None] + orders[:, None] * jnp.log(sine_theta)[None, :])
    blanks = jnp.zeros_like(diagonal_term)
    legendre = jnp.zeros((orders.shape[0], degrees, sine_theta.shape[0]), diagonal_term.dtype)

    def block_step(block_index, state_tuple):
        previous, earlier, legendre = state_tuple
        values = []
        for offset in range(8):
            degree = (block_index * 8 + offset).astype(diagonal_term.dtype)
            square = degree * degree
            upper_ratio = jnp.sqrt(jnp.maximum(4.0 * square - 1.0, 1.0) / jnp.maximum(square - orders * orders, 1.0))
            below_sq = (degree - 1.0) * (degree - 1.0)
            lower_ratio = jnp.sqrt(jnp.maximum(below_sq - orders * orders, 0.0) / jnp.maximum(4.0 * below_sq - 1.0, 1.0))
            recurred = upper_ratio[:, None] * (cosine[None, :] * previous - lower_ratio[:, None] * earlier)
            current = jnp.where((degree < orders)[:, None], blanks, jnp.where((degree == orders)[:, None], diagonal_term, recurred))
            values.append(current)
            earlier = previous
            previous = current
        stacked = jnp.stack(values, axis=1)
        legendre = lax.dynamic_update_slice(legendre, stacked, (jnp.int32(0), (block_index * 8).astype(jnp.int32), jnp.int32(0)))
        return (previous, earlier, legendre)
    return lax.fori_loop(0, degrees // 8, block_step, (blanks, blanks, legendre))[2]

def fourier_tables(lon_count, mode_count, float_type):
    product_index = jnp.arange(lon_count).astype(jnp.int32)[:, None] * jnp.arange(mode_count).astype(jnp.int32)[None, :] % lon_count
    phase_grid = 2.0 * jnp.pi * product_index.astype(float_type) / lon_count
    forward = jnp.stack([jnp.cos(phase_grid), -jnp.sin(phase_grid)], axis=1) / lon_count
    factor = jnp.where(jnp.arange(mode_count).astype(jnp.int32) == 0, 1.0, 2.0).astype(float_type)
    inverse = jnp.stack([jnp.cos(phase_grid).T * factor[:, None], -jnp.sin(phase_grid).T * factor[:, None]], axis=0)
    return (forward, inverse)

def harmonic_filter(latent, filter_gains):
    lat_count, lon_count = (latent.shape[0], latent.shape[1])
    mode_count = filter_gains.shape[0]
    forward, inverse = fourier_tables(lon_count, mode_count, jnp.float32)
    colat_grid = colatitude(lat_count, jnp.float32)
    orders = jnp.arange(mode_count).astype(jnp.int32).astype(jnp.float32)
    legendre = legendre_table(orders, mode_count, jnp.cos(colat_grid), jnp.sin(colat_grid))
    quadrature = 2.0 * jnp.pi * jnp.pi * jnp.sin(colat_grid) / lat_count
    weighted = legendre * quadrature
    coeffs = jnp.einsum('inc,nrk->irkc', latent, forward, precision=highest)
    spectrum = jnp.einsum('kli,irkc->lrkc', weighted, coeffs, precision=highest)
    spectrum = spectrum * filter_gains[:, None, None, :]
    restored = jnp.einsum('kli,lrkc->irkc', legendre, spectrum, precision=highest)
    return jnp.einsum('irkc,rkn->inc', restored, inverse, precision=highest)

def channel_mlp(latent, norm_gain, up_weight, down_weight):
    average = lax.optimization_barrier(jnp.mean(latent, axis=-1, keepdims=True))
    centred = latent - average
    spread = lax.optimization_barrier(jnp.mean(centred * centred, axis=-1, keepdims=True))
    normed = (centred * lax.rsqrt(spread + 1e-05) * norm_gain).astype(jnp.bfloat16)
    hidden = jnp.dot(normed, up_weight, preferred_element_type=jnp.float32)
    active = jax.nn.gelu(hidden, approximate=True).astype(jnp.bfloat16)
    return latent + jnp.dot(active, down_weight, preferred_element_type=jnp.float32)

def reference(latent, conv_first, conv_second, filter_gains, norm_gain, up_weight, down_weight):
    after_first = latent + local_stencil(latent, conv_first)
    after_second = after_first + harmonic_filter(after_first, filter_gains)
    after_third = after_second + local_stencil(after_second, conv_second)
    return channel_mlp(after_third, norm_gain, up_weight, down_weight)
```

```python
import functools
import math

import jax
import jax.numpy as jnp
import numpy as np
from jax import lax
from jax.experimental import pallas as pl
from jax.experimental.pallas import tpu as pltpu
from jax.sharding import PartitionSpec as P

highest = lax.Precision.HIGHEST


def padded_2(block, sides, width):
    for axis, dim in sides:
        count = lax.axis_size(axis)
        forward = [(i, i + 1) for i in range(count - 1)]
        backward = [(target, source) for source, target in forward]
        low = lax.ppermute(
            lax.slice_in_dim(block, block.shape[dim] - width, None, axis=dim), axis, forward
        )
        high = lax.ppermute(lax.slice_in_dim(block, 0, width, axis=dim), axis, backward)
        block = jnp.concatenate([low, block, high], axis=dim)
    return block


def stencil_sum(padded, weights, row_count, col_count):
    stencil_total = jnp.zeros((row_count, col_count, padded.shape[2]), padded.dtype)
    for row_shift in range(5):
        for col_shift in range(5):
            stencil_total = (
                stencil_total
                + weights[row_shift * 5 + col_shift]
                * padded[row_shift : row_shift + row_count, col_shift : col_shift + col_count, :]
            )
    return stencil_total


def slice_stencil(sliced, weights):
    lat_extended = padded_2(sliced, (("lat", 0),), 2)
    wrapped = jnp.concatenate([lat_extended[:, -2:], lat_extended, lat_extended[:, :2]], axis=1)
    return stencil_sum(wrapped, weights, sliced.shape[0], sliced.shape[1])


def colatitude(cell_count, float_type):
    cell_index = jnp.arange(cell_count).astype(float_type)
    return jnp.pi * (cell_index + 0.5) / cell_count


def legendre_table(orders, degrees, cosine, sine_theta):
    log_seed = 0.5 * (
        jnp.log((2.0 * orders + 1.0) / (4.0 * jnp.pi))
        + jax.scipy.special.gammaln(2.0 * orders + 1.0)
        - 2.0 * orders * jnp.log(2.0)
        - 2.0 * jax.scipy.special.gammaln(orders + 1.0)
    )
    diagonal_term = jnp.exp(log_seed[:, None] + orders[:, None] * jnp.log(sine_theta)[None, :])
    blanks = jnp.zeros_like(diagonal_term)
    legendre = jnp.zeros((orders.shape[0], degrees, sine_theta.shape[0]), diagonal_term.dtype)

    def block_step(block_index, state_tuple):
        previous, earlier, legendre = state_tuple
        values = []
        for offset in range(8):
            degree = (block_index * 8 + offset).astype(diagonal_term.dtype)
            square = degree * degree
            upper_ratio = jnp.sqrt(
                jnp.maximum(4.0 * square - 1.0, 1.0) / jnp.maximum(square - orders * orders, 1.0)
            )
            below_sq = (degree - 1.0) * (degree - 1.0)
            lower_ratio = jnp.sqrt(
                jnp.maximum(below_sq - orders * orders, 0.0)
                / jnp.maximum(4.0 * below_sq - 1.0, 1.0)
            )
            recurred = upper_ratio[:, None] * (
                cosine[None, :] * previous - lower_ratio[:, None] * earlier
            )
            current = jnp.where(
                (degree < orders)[:, None],
                blanks,
                jnp.where((degree == orders)[:, None], diagonal_term, recurred),
            )
            values.append(current)
            earlier = previous
            previous = current
        stacked = jnp.stack(values, axis=1)
        legendre = lax.dynamic_update_slice(
            legendre, stacked, (jnp.int32(0), (block_index * 8).astype(jnp.int32), jnp.int32(0))
        )
        return (previous, earlier, legendre)

    return lax.fori_loop(0, degrees // 8, block_step, (blanks, blanks, legendre))[2]


def fourier_tables(lon_count, mode_count, float_type):
    product_index = jnp.arange(lon_count)[:, None] * jnp.arange(mode_count)[None, :] % lon_count
    phase_grid = 2.0 * jnp.pi * product_index.astype(float_type) / lon_count
    forward = jnp.stack([jnp.cos(phase_grid), -jnp.sin(phase_grid)], axis=1) / lon_count
    factor = jnp.where(jnp.arange(mode_count) == 0, 1.0, 2.0).astype(float_type)
    inverse = jnp.stack(
        [jnp.cos(phase_grid).T * factor[:, None], -jnp.sin(phase_grid).T * factor[:, None]], axis=0
    )
    return (forward, inverse)


def channel_mlp(latent, norm_gain, up_weight, down_weight):
    average = jnp.mean(latent, axis=-1, keepdims=True)
    centred = latent - average
    spread = jnp.mean(centred * centred, axis=-1, keepdims=True)
    normed = (centred * lax.rsqrt(spread + 1e-05) * norm_gain).astype(jnp.bfloat16)
    hidden = jnp.dot(normed, up_weight, preferred_element_type=jnp.float32)
    active = jax.nn.gelu(hidden, approximate=True).astype(jnp.bfloat16)
    return latent + jnp.dot(active, down_weight, preferred_element_type=jnp.float32)


def per_device(latent, conv_first, conv_second, filter_gains, norm_gain, up_weight, down_weight):
    lat_size = lax.axis_size("lat")
    lon_size = lax.axis_size("lon")
    lat_local = latent.shape[0]
    lon_local = latent.shape[1]
    slice_width = filter_gains.shape[1]
    mode_count = filter_gains.shape[0]
    lat_count = lat_local * lat_size
    lon_count = lon_local * lon_size
    order_count = mode_count // lat_size
    channel_start = lax.axis_index("lon") * slice_width
    sliced = lax.all_to_all(latent, "lon", split_axis=2, concat_axis=1, tiled=True)
    first_taps = lax.dynamic_slice_in_dim(conv_first, channel_start, slice_width, 1)
    first_sliced = sliced + slice_stencil(sliced, first_taps)
    forward, inverse = fourier_tables(lon_count, mode_count, jnp.float32)
    colat_grid = colatitude(lat_count, jnp.float32)
    orders = (lax.axis_index("lat") * order_count + jnp.arange(order_count)).astype(jnp.float32)
    legendre = legendre_table(orders, mode_count, jnp.cos(colat_grid), jnp.sin(colat_grid))
    quadrature = 2.0 * jnp.pi * jnp.pi * jnp.sin(colat_grid) / lat_count
    weighted = legendre * quadrature
    coeffs = jnp.einsum("inc,nrk->irkc", first_sliced, forward, precision=highest)
    spectrum = jnp.einsum(
        "kli,irkc->lrkc",
        weighted,
        lax.all_to_all(coeffs, "lat", split_axis=2, concat_axis=0, tiled=True),
        precision=highest,
    )
    spectrum = spectrum * filter_gains[:, None, None, :]
    restored = jnp.einsum("kli,lrkc->irkc", legendre, spectrum, precision=highest)
    returned = lax.all_to_all(restored, "lat", split_axis=0, concat_axis=2, tiled=True)
    filtered = jnp.einsum("irkc,rkn->inc", returned, inverse, precision=highest)
    second_taps = lax.dynamic_slice_in_dim(conv_second, channel_start, slice_width, 1)
    second_sliced = first_sliced + filtered
    incoming = second_sliced + slice_stencil(second_sliced, second_taps)
    arrived = lax.all_to_all(incoming, "lon", split_axis=1, concat_axis=2, tiled=True)
    return channel_mlp(arrived, norm_gain, up_weight, down_weight)


LANES = 128
TILE = 8
GROUP = 4
SLOT = LANES // GROUP
HALF = LANES // 2
bf16 = jnp.bfloat16
f32 = jnp.float32


def legendre_numpy(modes, lat_count):
    theta = np.pi * (np.arange(lat_count) + 0.5) / lat_count
    cosine, sine = np.cos(theta), np.sin(theta)
    table = np.zeros((modes, modes, lat_count))
    for m in range(modes):
        seed = 0.5 * (
            math.log((2 * m + 1) / (4 * math.pi))
            + math.lgamma(2 * m + 1)
            - 2 * m * math.log(2.0)
            - 2 * math.lgamma(m + 1)
        )
        table[m, m] = np.exp(seed + m * np.log(sine))
        for l in range(m + 1, modes):
            a = math.sqrt((4.0 * l * l - 1) / (l * l - m * m))
            b = math.sqrt(max((l - 1.0) ** 2 - m * m, 0.0) / (4.0 * (l - 1.0) ** 2 - 1)) if l > 1 else 0.0
            earlier = table[m, l - 2] if l > m + 1 else 0.0
            table[m, l] = a * (cosine * table[m, l - 1] - b * earlier)
    quadrature = 2 * np.pi**2 * sine / lat_count
    return table, table * quadrature


def split_numpy(table):
    high = table.astype(np.float32).astype(jnp.bfloat16)
    low = (table - high.astype(np.float64)).astype(np.float32).astype(jnp.bfloat16)
    return high, low


@functools.lru_cache(maxsize=None)
def constant_tables(lat_count, lon_count, modes):
    pairs = modes // 2
    n = np.arange(lon_count)
    k = np.arange(modes)
    phase = 2 * np.pi * ((k[:, None] * n[None, :]) % lon_count) / lon_count
    trig = np.stack([np.cos(phase), -np.sin(phase)], axis=1)
    by_row = trig.reshape(2, pairs, 2, lon_count).transpose(0, 2, 1, 3).reshape(2 * modes, lon_count)
    forward = np.zeros((2 * modes, LANES))
    forward[:, :lon_count] = by_row / lon_count
    high, low = split_numpy(forward)
    forward = np.concatenate([high, high, low], axis=1)
    factor = np.where(k == 0, 1.0, 2.0)
    scaled = (trig * factor[:, None, None]).reshape(2, pairs, 2, lon_count).transpose(0, 2, 1, 3)
    scaled = scaled.reshape(2 * modes, lon_count)
    back = np.zeros((LANES, LANES))
    back[: 2 * modes, :lon_count] = scaled
    back[: 2 * modes, lon_count : lon_count + 2] = scaled[:, :2]
    back[: 2 * modes, LANES - 2 :] = scaled[:, lon_count - 2 :]
    high, low = split_numpy(back)
    back = np.concatenate([high, high, low], axis=0)
    table, weighted = legendre_numpy(modes, lat_count)
    into = np.zeros((pairs, LANES, LANES))
    onto = np.zeros((pairs, LANES, LANES))
    for s in range(2):
        part = slice(s * pairs, (s + 1) * pairs)
        lat, deg = slice(s * HALF, s * HALF + lat_count), slice(s * HALF, s * HALF + modes)
        into[:, lat, deg] = np.swapaxes(weighted[part], 1, 2)
        onto[:, deg, lat] = table[part]
    into = np.concatenate(split_numpy(into), axis=2)
    onto = np.concatenate(split_numpy(onto), axis=2)
    return forward, back, into, onto


def halves(value):
    high = value.astype(bf16)
    return high, (value - high.astype(f32)).astype(bf16)


def mm(a, b):
    return jnp.dot(a, b, preferred_element_type=f32)


def mm_wide(value, table):
    count = value.shape[0]
    high, low = halves(value)
    out = mm(jnp.concatenate([high, low], axis=0), table)
    return (out[:count, :LANES] + out[count:, :LANES]) + (out[:count, LANES:] + out[count:, LANES:])


def chunk_list(per):
    chunks = [(start, TILE) for start in range(0, per - per % TILE, TILE)]
    if per % TILE:
        chunks.append((per - per % TILE, per % TILE))
    return chunks


def block_kernel(
    nl, nj, rows, modes,
    latent, conv_first, conv_second, gains, norm_gain, fwd_hbm, back_hbm, into_hbm, onto_hbm, up_hbm, down_hbm,
    out,
    grid, sent, got, field, first, second, spec_in, spec_out, back_out, home, third,
    tap_one, tap_two, tap_col, taps, gain_in, gain_wide, gain_col, norm_in, fwd, back, into, onto, up, down,
    load_sem, in_sem, out_sem, own_a, own_z, a_s, a_r, z_s, z_r,
):
    channels = latent.shape[1]
    cols = latent.shape[0] // rows
    blocks = channels // LANES
    total = nl * nj
    per = channels // total
    chunks = chunk_list(per)
    halves_count = rows // GROUP
    lat_count = rows * nl
    lon_count = cols * nj
    pairs = modes // 2
    la, lo = lax.axis_index("lat"), lax.axis_index("lon")
    me = lo * nl + la

    def lanes(block):
        return pl.ds(block * LANES, LANES)

    def tile(start):
        return pl.ds(start if isinstance(start, int) else pl.multiple_of(start, TILE), TILE)

    def rcopy(src, dst, send, recv, a, b):
        return pltpu.make_async_remote_copy(
            src_ref=src, dst_ref=dst, send_sem=send, recv_sem=recv,
            device_id={"lat": a, "lon": b}, device_id_type=pl.DeviceIdType.MESH,
        )

    def others(action):
        for d in range(1, nj):
            action(la, lax.rem(lo + d, nj))

        def step(d, carry):
            a = lax.rem(la + d, nl)
            for b in range(nj):
                action(a, lax.rem(lo + b, nj))
            return carry

        lax.fori_loop(1, nl, step, 0)

    barrier = pltpu.get_barrier_semaphore()
    others(
        lambda a, b: pl.semaphore_signal(
            barrier, inc=1, device_id={"lat": a, "lon": b}, device_id_type=pl.DeviceIdType.MESH
        )
    )

    pairs_of = (
        (conv_first, tap_one), (conv_second, tap_two), (gains, gain_in),
        (norm_gain, norm_in), (fwd_hbm, fwd), (back_hbm, back), (into_hbm, into), (onto_hbm, onto),
        (up_hbm, up), (down_hbm, down),
    )
    loads = [pltpu.make_async_copy(a, b, load_sem.at[i]) for i, (a, b) in enumerate(pairs_of)]

    def in_copy(block):
        return pltpu.make_async_copy(
            latent.at[:, lanes(block)], grid.at[block, pl.ds(0, rows * cols)], in_sem.at[block]
        )

    def out_copy(block):
        return pltpu.make_async_copy(
            grid.at[block, pl.ds(0, rows * cols)], out.at[:, lanes(block)], out_sem.at[block]
        )

    for block in range(blocks):
        in_copy(block).start()
    for load in loads:
        load.start()

    for block in range(blocks):
        grid[block, rows * cols :, :] = jnp.zeros((rows * (SLOT - cols), LANES), f32)
    empty = jnp.zeros((2 * TILE, LANES), f32)
    for padded in (field, second):
        for k in range(len(chunks)):
            padded[k, 0 : 2 * TILE, :] = empty
            padded[k, (lat_count + 2) * TILE : (lat_count + 4) * TILE, :] = empty

    for block in range(blocks):
        in_copy(block).wait()
        for h in range(halves_count):
            parts = [grid[block, pl.ds(h * GROUP + i, SLOT, stride=rows), :] for i in range(GROUP)]
            sent[h, lanes(block), :] = jnp.concatenate(parts, axis=0).T

    def a_copy(k, a, b):
        start, count = chunks[k]
        return rcopy(
            sent.at[:, pl.ds((b * nl + a) * per + start, count), :],
            got.at[la, lo, :, pl.ds(start, count), :],
            a_s.at[k], a_r.at[k], a, b,
        )

    def z_copy(k, a, b):
        start, count = chunks[k]
        return rcopy(
            back_out.at[a, b, :, pl.ds(start, count), :],
            home.at[:, pl.ds(me * per + start, count), :],
            z_s.at[k], z_r.at[k], a, b,
        )

    def own_in(k):
        start, count = chunks[k]
        return pltpu.make_async_copy(
            sent.at[:, pl.ds(me * per + start, count), :], got.at[la, lo, :, pl.ds(start, count), :], own_a.at[k]
        )

    def own_back(k):
        start, count = chunks[k]
        return pltpu.make_async_copy(
            back_out.at[la, lo, :, pl.ds(start, count), :], home.at[:, pl.ds(me * per + start, count), :], own_z.at[k]
        )

    def everyone(k, send, recv):
        whole = first.at[0, pl.ds(0, (total - 1) * halves_count * chunks[k][1])]
        return rcopy(whole, whole, send.at[k], recv.at[k], lax.rem(la + 1, nl), lo)

    pl.semaphore_wait(barrier, total - 1)
    for k in range(len(chunks)):
        others(lambda a, b, k=k: a_copy(k, a, b).start())
        own_in(k).start()

    loads[0].wait()
    loads[1].wait()
    loads[2].wait()
    gain_wide[...] = jnp.zeros_like(gain_wide)
    gain_wide[0:modes, :] = gain_in[...]
    gain_wide[HALF : HALF + modes, :] = gain_in[...]
    width = gain_in.shape[1]
    for start in range(0, width, LANES):
        stop = min(start + LANES, width)
        gain_col[start:stop, :] = gain_wide[:, start:stop].T
    for s, source in enumerate((tap_one, tap_two)):
        for block in range(blocks):
            square = jnp.concatenate([source[:, lanes(block)], jnp.zeros((7, LANES), f32)], axis=0)
            tap_col[s, lanes(block), :] = square.T
        for k, (start, _) in enumerate(chunks):
            own = tap_col[s, pl.ds(me * per + start, TILE), :]
            for t in range(25):
                taps[s, k, t] = jnp.broadcast_to(own[:, t : t + 1], (TILE, LANES))

    lane = lax.broadcasted_iota(jnp.int32, (TILE, LANES), 1)
    low_half = lax.broadcasted_iota(jnp.int32, (pairs, LANES), 1) < HALF

    def wrap(row):
        row = jnp.where(lane >= lon_count, pltpu.roll(row, lon_count, 1), row)
        return jnp.where(lane >= LANES - 2, pltpu.roll(row, LANES - lon_count, 1), row)

    def unpack(k):
        start = chunks[k][0]

        def step(a, carry):
            for h in range(halves_count):
                pieces = [got[a, b, h, tile(start), :] for b in range(nj)]
                for i in range(GROUP):
                    row = None
                    for b in reversed(range(nj)):
                        shift = (cols * b - SLOT * i) % LANES
                        moved = pltpu.roll(pieces[b], shift, 1) if shift else pieces[b]
                        row = moved if row is None else jnp.where(lane < cols * (b + 1), moved, row)
                    field[k, tile((a * rows + h * GROUP + i + 2) * TILE), :] = wrap(row)
            return carry

        lax.fori_loop(0, nl, step, 0)

    def stencil(source, s, k, emit):
        step_rows = TILE

        def step(g, carry):
            base = g * step_rows
            lines = [source[k, tile((base + j) * TILE), :] for j in range(step_rows + 4)]
            sums = [lines[j + 2] for j in range(step_rows)]
            for b in range(5):
                weights = [taps[s, k, a * 5 + b] for a in range(5)]
                for j in range(step_rows):
                    term = weights[0] * lines[j]
                    for a in range(1, 5):
                        term = term + weights[a] * lines[j + a]
                    if b != 2:
                        term = pltpu.roll(term, (2 - b) % LANES, 1)
                    sums[j] = sums[j] + term
            emit(g, base, sums)
            return carry

        lax.fori_loop(0, lat_count // step_rows, step, 0)

    def transform(k):
        count = chunks[k][1]
        by_channel = jnp.concatenate(
            [first[k, pl.ds(c, lat_count, stride=TILE), :] for c in range(count)], axis=0
        )
        high, low = halves(by_channel)
        coeffs = lax.dot_general(
            fwd[...], jnp.concatenate([high, low, high], axis=1), (((1,), (1,)), ((), ())),
            preferred_element_type=f32,
        )
        for p in range(count // 2):
            for r in range(2):
                part = [coeffs[(2 * s + r) * pairs : (2 * s + r + 1) * pairs, lanes_of(p)] for s in range(2)]
                even = jnp.where(low_half, part[0], pltpu.roll(part[1], HALF, 1))
                odd = jnp.where(low_half, pltpu.roll(part[0], HALF, 1), part[1])
                spec_in[k, pl.ds(r * TILE + 2 * p, pairs, stride=2 * TILE), :] = even
                spec_in[k, pl.ds(r * TILE + 2 * p + 1, pairs, stride=2 * TILE), :] = odd

    def lanes_of(p):
        return slice(p * LANES, (p + 1) * LANES)

    def degrees(k):
        gain = gain_col[pl.ds(la * per + chunks[k][0], TILE), :]
        gain = jnp.concatenate([gain, gain], axis=0)
        for m in range(pairs):
            at = pl.ds(m * 2 * TILE, 2 * TILE)
            spectrum = mm_wide(spec_in[k, at, :], into[m]) * gain
            spec_out[k, at, :] = mm_wide(spectrum, onto[m])

    def synthesis(k):
        count = chunks[k][1]
        rows_of = [[None] * (count // 2) for _ in range(4)]
        for p in range(count // 2):
            for r in range(2):
                even = spec_out[k, pl.ds(r * TILE + 2 * p, pairs, stride=2 * TILE), :]
                odd = spec_out[k, pl.ds(r * TILE + 2 * p + 1, pairs, stride=2 * TILE), :]
                rows_of[r][p] = jnp.where(low_half, even, pltpu.roll(odd, HALF, 1))
                rows_of[2 + r][p] = jnp.where(low_half, pltpu.roll(even, HALF, 1), odd)
        blank = jnp.zeros((LANES - 4 * pairs, LANES), f32)
        for p in range(count // 2):
            square = jnp.concatenate([rows_of[q][p] for q in range(4)] + [blank], axis=0).T
            high, low = halves(square)
            values = mm(jnp.concatenate([high, low, high], axis=1), back[...])
            for e in range(2):
                at = 2 * p + e
                before = first[k, pl.ds(at, lat_count, stride=TILE), :]
                second[k, pl.ds(2 * TILE + at, lat_count, stride=TILE), :] = (
                    before + values[e * lat_count : (e + 1) * lat_count]
                )

    def emit_first(k):
        def emit(g, base, sums):
            for j, row in enumerate(sums):
                first[k, tile((base + j) * TILE), :] = wrap(row)
        return emit

    def emit_second(k):
        start = chunks[k][0]

        def emit(a, base, sums):
            for h in range(halves_count):
                for b in range(nj):
                    packed = None
                    for i in reversed(range(GROUP)):
                        shift = (SLOT * i - cols * b) % LANES
                        row = sums[h * GROUP + i]
                        moved = pltpu.roll(row, shift, 1) if shift else row
                        packed = moved if packed is None else jnp.where(lane < SLOT * (i + 1), moved, packed)
                    back_out[a, b, h, tile(start), :] = packed
        return emit

    for k in range(len(chunks)):
        everyone(k, a_s, a_r).wait_recv()
        own_in(k).wait()
        unpack(k)
        stencil(field, 0, k, emit_first(k))
        if k == 0:
            loads[4].wait()
        transform(k)
        if k == 0:
            loads[6].wait()
            loads[7].wait()
        degrees(k)
        if k == 0:
            loads[5].wait()
        synthesis(k)
        stencil(second, 1, k, emit_second(k))
        others(lambda a, b, k=k: z_copy(k, a, b).start())
        own_back(k).start()

    loads[3].wait()
    loads[8].wait()
    loads[9].wait()
    for k in range(len(chunks)):
        everyone(k, z_s, z_r).wait_recv()
        own_back(k).wait()
    for h in range(halves_count):
        for block in range(blocks):
            third[pl.ds(h * LANES, LANES), lanes(block)] = home[h, lanes(block), :].T
    state = third[...]
    average = jnp.mean(state, axis=-1, keepdims=True)
    centred = state - average
    spread = jnp.mean(centred * centred, axis=-1, keepdims=True)
    normed = (centred * lax.rsqrt(spread + 1e-05) * norm_in[...].reshape(1, channels)).astype(bf16)
    active = jax.nn.gelu(mm(normed, up[...]), approximate=True).astype(bf16)
    third[...] = state + mm(active, down[...])
    for block in range(blocks):
        for i in range(rows):
            grid[block, pl.ds(i, cols, stride=rows), :] = third[SLOT * i : SLOT * i + cols, lanes(block)]
        out_copy(block).start()
    for block in range(blocks):
        out_copy(block).wait()
    for k in range(len(chunks)):
        everyone(k, a_s, a_r).wait_send()
        everyone(k, z_s, z_r).wait_send()


def fused(nl, nj, latent, conv_first, conv_second, filter_gains, norm_gain, up_weight, down_weight):
    rows, cols, channels = latent.shape
    modes, width = filter_gains.shape
    lat_count, lon_count = rows * nl, cols * nj
    forward, back, into, onto = (jnp.asarray(t) for t in constant_tables(lat_count, lon_count, modes))
    blocks = channels // LANES
    per = channels // (nl * nj)
    count = len(chunk_list(per))
    room = count * TILE
    halves_count = rows // GROUP
    vm = lambda *shape, kind=f32: pltpu.VMEM(shape, kind)
    dma = lambda *shape: pltpu.SemaphoreType.DMA(shape)
    far = pl.BlockSpec(memory_space=pltpu.HBM)
    result = pl.pallas_call(
        functools.partial(block_kernel, nl, nj, rows, modes),
        out_shape=jax.ShapeDtypeStruct((cols * rows, channels), f32),
        in_specs=[far] * 11,
        out_specs=far,
        scratch_shapes=[
            vm(blocks, rows * SLOT, LANES),
            vm(halves_count, channels, LANES),
            vm(nl, nj, halves_count, room, LANES),
            vm(count, (lat_count + 4) * TILE, LANES),
            vm(count, lat_count * TILE, LANES),
            vm(count, (lat_count + 4) * TILE, LANES),
            vm(count, modes * TILE, LANES),
            vm(count, modes * TILE, LANES),
            vm(nl, nj, halves_count, room, LANES),
            vm(halves_count, channels, LANES),
            vm(rows * SLOT, channels),
            vm(25, channels),
            vm(25, channels),
            vm(2, channels + TILE, 32),
            vm(2, count, 25, TILE, LANES),
            vm(modes, width),
            vm(LANES, width),
            vm(width + TILE, LANES),
            vm(channels),
            vm(*forward.shape, kind=bf16),
            vm(*back.shape, kind=bf16),
            vm(*into.shape, kind=bf16),
            vm(*onto.shape, kind=bf16),
            vm(*up_weight.shape, kind=bf16),
            vm(*down_weight.shape, kind=bf16),
            dma(10), dma(blocks), dma(blocks), dma(count), dma(count),
            dma(count), dma(count), dma(count), dma(count),
        ],
        compiler_params=pltpu.CompilerParams(
            collective_id=0, has_side_effects=True, vmem_limit_bytes=60 * 1024 * 1024
        ),
        name="block",
    )(
        jnp.swapaxes(latent, 0, 1).reshape(cols * rows, channels), conv_first, conv_second,
        filter_gains, norm_gain, forward, back, into, onto, up_weight, down_weight,
    )
    return jnp.swapaxes(result.reshape(cols, rows, channels), 0, 1)


def fits(nl, nj, latent, filter_gains):
    rows, cols, channels = latent.shape
    modes = filter_gains.shape[0]
    total = nl * nj
    if rows != TILE or channels % LANES or channels % total or nj < 2 or nl < 2:
        return False
    if (channels // total) % 4 or rows * nl != HALF or cols > SLOT or cols * nj > LANES - 4:
        return False
    return modes % 16 == 0 and modes <= HALF and 2 * modes <= LANES


def body(latent, conv_first, conv_second, filter_gains, norm_gain, up_weight, down_weight):
    nl, nj = lax.axis_size("lat"), lax.axis_size("lon")
    arguments = (latent, conv_first, conv_second, filter_gains, norm_gain, up_weight, down_weight)
    if fits(nl, nj, latent, filter_gains):
        return fused(nl, nj, *arguments)
    return per_device(*arguments)


def solution(mesh):
    return jax.shard_map(
        body,
        mesh=mesh,
        in_specs=(P("lat", "lon", None), P(), P(), P(None, "lon"), P(), P(), P()),
        out_specs=P("lat", "lon", None),
        check_vma=False,
    )
```

```python
import functools
import math

import jax
import jax.numpy as jnp
import numpy as np
from jax import lax
from jax.experimental import pallas as pl
from jax.experimental.pallas import tpu as pltpu
from jax.sharding import PartitionSpec as P

highest = lax.Precision.HIGHEST


def padded_2(block, sides, width):
    for axis, dim in sides:
        count = lax.axis_size(axis)
        forward = [(i, i + 1) for i in range(count - 1)]
        backward = [(target, source) for source, target in forward]
        low = lax.ppermute(
            lax.slice_in_dim(block, block.shape[dim] - width, None, axis=dim), axis, forward
        )
        high = lax.ppermute(lax.slice_in_dim(block, 0, width, axis=dim), axis, backward)
        block = jnp.concatenate([low, block, high], axis=dim)
    return block


def stencil_sum(padded, weights, row_count, col_count):
    stencil_total = jnp.zeros((row_count, col_count, padded.shape[2]), padded.dtype)
    for row_shift in range(5):
        for col_shift in range(5):
            stencil_total = (
                stencil_total
                + weights[row_shift * 5 + col_shift]
                * padded[row_shift : row_shift + row_count, col_shift : col_shift + col_count, :]
            )
    return stencil_total


def slice_stencil(sliced, weights):
    lat_extended = padded_2(sliced, (("lat", 0),), 2)
    wrapped = jnp.concatenate([lat_extended[:, -2:], lat_extended, lat_extended[:, :2]], axis=1)
    return stencil_sum(wrapped, weights, sliced.shape[0], sliced.shape[1])


def colatitude(cell_count, float_type):
    cell_index = jnp.arange(cell_count).astype(float_type)
    return jnp.pi * (cell_index + 0.5) / cell_count


def legendre_table(orders, degrees, cosine, sine_theta):
    log_seed = 0.5 * (
        jnp.log((2.0 * orders + 1.0) / (4.0 * jnp.pi))
        + jax.scipy.special.gammaln(2.0 * orders + 1.0)
        - 2.0 * orders * jnp.log(2.0)
        - 2.0 * jax.scipy.special.gammaln(orders + 1.0)
    )
    diagonal_term = jnp.exp(log_seed[:, None] + orders[:, None] * jnp.log(sine_theta)[None, :])
    blanks = jnp.zeros_like(diagonal_term)
    legendre = jnp.zeros((orders.shape[0], degrees, sine_theta.shape[0]), diagonal_term.dtype)

    def block_step(block_index, state_tuple):
        previous, earlier, legendre = state_tuple
        values = []
        for offset in range(8):
            degree = (block_index * 8 + offset).astype(diagonal_term.dtype)
            square = degree * degree
            upper_ratio = jnp.sqrt(
                jnp.maximum(4.0 * square - 1.0, 1.0) / jnp.maximum(square - orders * orders, 1.0)
            )
            below_sq = (degree - 1.0) * (degree - 1.0)
            lower_ratio = jnp.sqrt(
                jnp.maximum(below_sq - orders * orders, 0.0)
                / jnp.maximum(4.0 * below_sq - 1.0, 1.0)
            )
            recurred = upper_ratio[:, None] * (
                cosine[None, :] * previous - lower_ratio[:, None] * earlier
            )
            current = jnp.where(
                (degree < orders)[:, None],
                blanks,
                jnp.where((degree == orders)[:, None], diagonal_term, recurred),
            )
            values.append(current)
            earlier = previous
            previous = current
        stacked = jnp.stack(values, axis=1)
        legendre = lax.dynamic_update_slice(
            legendre, stacked, (jnp.int32(0), (block_index * 8).astype(jnp.int32), jnp.int32(0))
        )
        return (previous, earlier, legendre)

    return lax.fori_loop(0, degrees // 8, block_step, (blanks, blanks, legendre))[2]


def fourier_tables(lon_count, mode_count, float_type):
    product_index = jnp.arange(lon_count)[:, None] * jnp.arange(mode_count)[None, :] % lon_count
    phase_grid = 2.0 * jnp.pi * product_index.astype(float_type) / lon_count
    forward = jnp.stack([jnp.cos(phase_grid), -jnp.sin(phase_grid)], axis=1) / lon_count
    factor = jnp.where(jnp.arange(mode_count) == 0, 1.0, 2.0).astype(float_type)
    inverse = jnp.stack(
        [jnp.cos(phase_grid).T * factor[:, None], -jnp.sin(phase_grid).T * factor[:, None]], axis=0
    )
    return (forward, inverse)


def channel_mlp(latent, norm_gain, up_weight, down_weight):
    average = jnp.mean(latent, axis=-1, keepdims=True)
    centred = latent - average
    spread = jnp.mean(centred * centred, axis=-1, keepdims=True)
    normed = (centred * lax.rsqrt(spread + 1e-05) * norm_gain).astype(jnp.bfloat16)
    hidden = jnp.dot(normed, up_weight, preferred_element_type=jnp.float32)
    active = jax.nn.gelu(hidden, approximate=True).astype(jnp.bfloat16)
    return latent + jnp.dot(active, down_weight, preferred_element_type=jnp.float32)


def per_device(latent, conv_first, conv_second, filter_gains, norm_gain, up_weight, down_weight):
    lat_size = lax.axis_size("lat")
    lon_size = lax.axis_size("lon")
    lat_local = latent.shape[0]
    lon_local = latent.shape[1]
    slice_width = filter_gains.shape[1]
    mode_count = filter_gains.shape[0]
    lat_count = lat_local * lat_size
    lon_count = lon_local * lon_size
    order_count = mode_count // lat_size
    channel_start = lax.axis_index("lon") * slice_width
    sliced = lax.all_to_all(latent, "lon", split_axis=2, concat_axis=1, tiled=True)
    first_taps = lax.dynamic_slice_in_dim(conv_first, channel_start, slice_width, 1)
    first_sliced = sliced + slice_stencil(sliced, first_taps)
    forward, inverse = fourier_tables(lon_count, mode_count, jnp.float32)
    colat_grid = colatitude(lat_count, jnp.float32)
    orders = (lax.axis_index("lat") * order_count + jnp.arange(order_count)).astype(jnp.float32)
    legendre = legendre_table(orders, mode_count, jnp.cos(colat_grid), jnp.sin(colat_grid))
    quadrature = 2.0 * jnp.pi * jnp.pi * jnp.sin(colat_grid) / lat_count
    weighted = legendre * quadrature
    coeffs = jnp.einsum("inc,nrk->irkc", first_sliced, forward, precision=highest)
    spectrum = jnp.einsum(
        "kli,irkc->lrkc",
        weighted,
        lax.all_to_all(coeffs, "lat", split_axis=2, concat_axis=0, tiled=True),
        precision=highest,
    )
    spectrum = spectrum * filter_gains[:, None, None, :]
    restored = jnp.einsum("kli,lrkc->irkc", legendre, spectrum, precision=highest)
    returned = lax.all_to_all(restored, "lat", split_axis=0, concat_axis=2, tiled=True)
    filtered = jnp.einsum("irkc,rkn->inc", returned, inverse, precision=highest)
    second_taps = lax.dynamic_slice_in_dim(conv_second, channel_start, slice_width, 1)
    second_sliced = first_sliced + filtered
    incoming = second_sliced + slice_stencil(second_sliced, second_taps)
    arrived = lax.all_to_all(incoming, "lon", split_axis=1, concat_axis=2, tiled=True)
    return channel_mlp(arrived, norm_gain, up_weight, down_weight)


LANES = 128
TILE = 8
GROUP = 4
SLOT = LANES // GROUP
HALF = LANES // 2
bf16 = jnp.bfloat16
f32 = jnp.float32


def legendre_numpy(modes, lat_count):
    theta = np.pi * (np.arange(lat_count) + 0.5) / lat_count
    cosine, sine = np.cos(theta), np.sin(theta)
    table = np.zeros((modes, modes, lat_count))
    for m in range(modes):
        seed = 0.5 * (
            math.log((2 * m + 1) / (4 * math.pi))
            + math.lgamma(2 * m + 1)
            - 2 * m * math.log(2.0)
            - 2 * math.lgamma(m + 1)
        )
        table[m, m] = np.exp(seed + m * np.log(sine))
        for l in range(m + 1, modes):
            a = math.sqrt((4.0 * l * l - 1) / (l * l - m * m))
            b = math.sqrt(max((l - 1.0) ** 2 - m * m, 0.0) / (4.0 * (l - 1.0) ** 2 - 1)) if l > 1 else 0.0
            earlier = table[m, l - 2] if l > m + 1 else 0.0
            table[m, l] = a * (cosine * table[m, l - 1] - b * earlier)
    quadrature = 2 * np.pi**2 * sine / lat_count
    return table, table * quadrature


def split_numpy(table):
    high = table.astype(np.float32).astype(jnp.bfloat16)
    low = (table - high.astype(np.float64)).astype(np.float32).astype(jnp.bfloat16)
    return high, low


@functools.lru_cache(maxsize=None)
def constant_tables(lat_count, lon_count, modes):
    pairs = modes // 2
    n = np.arange(lon_count)
    k = np.arange(modes)
    phase = 2 * np.pi * ((k[:, None] * n[None, :]) % lon_count) / lon_count
    trig = np.stack([np.cos(phase), -np.sin(phase)], axis=1)
    by_row = trig.reshape(2, pairs, 2, lon_count).transpose(0, 2, 1, 3).reshape(2 * modes, lon_count)
    forward = np.zeros((2 * modes, LANES))
    forward[:, :lon_count] = by_row / lon_count
    high, low = split_numpy(forward)
    forward = np.concatenate([high, high, low], axis=1)
    factor = np.where(k == 0, 1.0, 2.0)
    scaled = (trig * factor[:, None, None]).reshape(2, pairs, 2, lon_count).transpose(0, 2, 1, 3)
    scaled = scaled.reshape(2 * modes, lon_count)
    back = np.zeros((LANES, LANES))
    back[: 2 * modes, :lon_count] = scaled
    back[: 2 * modes, lon_count : lon_count + 2] = scaled[:, :2]
    back[: 2 * modes, LANES - 2 :] = scaled[:, lon_count - 2 :]
    high, low = split_numpy(back)
    back = np.concatenate([high, high, low], axis=0)
    table, weighted = legendre_numpy(modes, lat_count)
    into = np.zeros((pairs, LANES, LANES))
    onto = np.zeros((pairs, LANES, LANES))
    for s in range(2):
        part = slice(s * pairs, (s + 1) * pairs)
        lat, deg = slice(s * HALF, s * HALF + lat_count), slice(s * HALF, s * HALF + modes)
        into[:, lat, deg] = np.swapaxes(weighted[part], 1, 2)
        onto[:, deg, lat] = table[part]
    into = np.concatenate(split_numpy(into), axis=2)
    onto = np.concatenate(split_numpy(onto), axis=2)
    return forward, back, into, onto


def halves(value):
    high = value.astype(bf16)
    return high, (value - high.astype(f32)).astype(bf16)


def mm(a, b):
    return jnp.dot(a, b, preferred_element_type=f32)


def mm_wide(value, table):
    count = value.shape[0]
    high, low = halves(value)
    out = mm(jnp.concatenate([high, low], axis=0), table)
    return (out[:count, :LANES] + out[count:, :LANES]) + (out[:count, LANES:] + out[count:, LANES:])


def chunk_list(per):
    chunks = [(start, TILE) for start in range(0, per - per % TILE, TILE)]
    if per % TILE:
        chunks.append((per - per % TILE, per % TILE))
    return chunks


def block_kernel(
    nl, nj, rows, modes,
    latent, conv_first, conv_second, gains, norm_gain, fwd_hbm, back_hbm, into_hbm, onto_hbm, up_hbm, down_hbm,
    out,
    grid, sent, got, field, first, second, spec_in, spec_out, back_out, home, third,
    tap_one, tap_two, tap_col, taps, gain_in, gain_wide, gain_col, norm_in, fwd, back, into, onto, up, down,
    load_sem, in_sem, out_sem, own_a, own_z, a_s, a_r, z_s, z_r,
):
    channels = latent.shape[1]
    cols = latent.shape[0] // rows
    blocks = channels // LANES
    total = nl * nj
    per = channels // total
    chunks = chunk_list(per)
    halves_count = rows // GROUP
    lat_count = rows * nl
    lon_count = cols * nj
    pairs = modes // 2
    la, lo = lax.axis_index("lat"), lax.axis_index("lon")
    me = lo * nl + la

    share = nl * per
    z_at, core = la // 2, lax.rem(la, 2)
    across = nl // 2

    def pieces_of(block):
        out, low = [], block * LANES
        while low < (block + 1) * LANES:
            high = min((block + 1) * LANES, (low // share + 1) * share)
            out.append((low // share, low, high))
            low = high
        return out

    def start_of(k, a):
        start, count = chunks[k]
        if per % TILE == 0:
            return a * per + start
        odd = lax.rem(a, 2)
        if count == TILE:
            return pl.multiple_of(a * per + odd * (per % TILE) + start, TILE)
        return a * per + (1 - odd) * start

    def channels_of(k, a, b):
        return (slice(None), b, pl.ds(start_of(k, a), chunks[k][1]), slice(None))

    def place_of(k, a, b):
        count = chunks[k][1]
        bands = nl * count // TILE
        return (lax.rem(a, bands), b, slice(None), pl.ds(k * TILE + a // bands * count, count), slice(None))

    def lanes(block):
        return pl.ds(block * LANES, LANES)

    def tile(start):
        return pl.ds(start if isinstance(start, int) else pl.multiple_of(start, TILE), TILE)

    def rcopy(src, dst, send, recv, a, b):
        return pltpu.make_async_remote_copy(
            src_ref=src, dst_ref=dst, send_sem=send, recv_sem=recv,
            device_id={"lat": a, "lon": b}, device_id_type=pl.DeviceIdType.MESH,
        )

    def others(action):
        for d in range(1, nj):
            action(la, lax.rem(lo + d, nj))

        def step(d, carry):
            a = lax.rem(la + d, nl)
            for b in range(nj):
                action(a, lax.rem(lo + b, nj))
            return carry

        lax.fori_loop(1, nl, step, 0)

    barrier = pltpu.get_barrier_semaphore()
    others(
        lambda a, b: pl.semaphore_signal(
            barrier, inc=1, device_id={"lat": a, "lon": b}, device_id_type=pl.DeviceIdType.MESH
        )
    )

    pairs_of = (
        (conv_first, tap_one), (conv_second, tap_two), (gains, gain_in),
        (norm_gain, norm_in), (fwd_hbm, fwd), (back_hbm, back), (into_hbm, into), (onto_hbm, onto),
        (up_hbm, up), (down_hbm, down),
    )
    loads = [pltpu.make_async_copy(a, b, load_sem.at[i]) for i, (a, b) in enumerate(pairs_of)]

    def in_copy(block):
        return pltpu.make_async_copy(
            latent.at[:, lanes(block)], grid.at[block, pl.ds(0, rows * cols)], in_sem.at[block]
        )

    def out_copy(block):
        return pltpu.make_async_copy(
            grid.at[block, pl.ds(0, rows * cols)], out.at[:, lanes(block)], out_sem.at[block]
        )

    for block in range(blocks):
        in_copy(block).start()
    for load in loads:
        load.start()

    for block in range(blocks):
        grid[block, rows * cols :, :] = jnp.zeros((rows * (SLOT - cols), LANES), f32)

    for block in range(blocks):
        in_copy(block).wait()
        for h in range(halves_count):
            parts = [grid[block, pl.ds(h * GROUP + i, SLOT, stride=rows), :] for i in range(GROUP)]
            block_rows = jnp.concatenate(parts, axis=0).T
            for b, low, high in pieces_of(block):
                sent[h, b, low - b * share : high - b * share, :] = block_rows[low - block * LANES : high - block * LANES]

    def a_copy(k, a, b):
        return rcopy(sent.at[channels_of(k, a, b)], got.at[place_of(k, la, lo)], a_s.at[k], a_r.at[k], a, b)

    def z_copy(k, a, b):
        return rcopy(back_out.at[place_of(k, a, b)], home.at[channels_of(k, la, lo)], z_s.at[k], z_r.at[k], a, b)

    def own_in(k):
        return pltpu.make_async_copy(sent.at[channels_of(k, la, lo)], got.at[place_of(k, la, lo)], own_a.at[k])

    def own_back(k):
        return pltpu.make_async_copy(back_out.at[place_of(k, la, lo)], home.at[channels_of(k, la, lo)], own_z.at[k])

    def everyone(k, send, recv):
        whole = first.at[0, pl.ds(0, (total - 1) * halves_count * chunks[k][1])]
        return rcopy(whole, whole, send.at[k], recv.at[k], lax.rem(la + 1, nl), lo)

    def spread(k, copy):
        def band(d, flip, start):
            a = lax.rem(z_at + d, across) * 2 + (1 - core if flip else core)
            for b in range(start, nj):
                copy(k, a, lax.rem(lo + b, nj)).start()

        for d in [0] + [e for q in range(1, across // 2 + 1) for e in sorted({q, across - q})]:
            band(d, False, 1 if d == 0 else 0)
            band(d, True, 0)

    pl.semaphore_wait(barrier, total - 1)
    def send_in(k):
        spread(k, a_copy)
        own_in(k).start()

    for k in range(len(chunks)):
        send_in(k)

    loads[0].wait()
    loads[1].wait()
    loads[2].wait()
    gain_wide[...] = jnp.zeros_like(gain_wide)
    gain_wide[0:modes, :] = gain_in[...]
    gain_wide[HALF : HALF + modes, :] = gain_in[...]
    width = gain_in.shape[1]
    for start in range(0, width, LANES):
        stop = min(start + LANES, width)
        gain_col[start:stop, :] = gain_wide[:, start:stop].T
    for s, source in enumerate((tap_one, tap_two)):
        for block in range(blocks):
            square = jnp.concatenate([source[:, lanes(block)], jnp.zeros((7, LANES), f32)], axis=0)
            tap_col[s, lanes(block), :] = square.T
        for k, (_, count) in enumerate(chunks):
            own = tap_col[s, pl.ds(lo * share + start_of(k, la), TILE), :]
            if count < TILE:
                own = jnp.concatenate([own[:count]] * (TILE // count), axis=0)
            for t in range(25):
                taps[s, k, t] = jnp.broadcast_to(own[:, t : t + 1], (TILE, LANES))

    lane = lax.broadcasted_iota(jnp.int32, (TILE, LANES), 1)
    sublane = lax.broadcasted_iota(jnp.int32, (TILE, LANES), 0)
    low_half = lax.broadcasted_iota(jnp.int32, (pairs, LANES), 1) < HALF

    def turned(row, shift):
        return pltpu.roll(row, shift % LANES, 1) if shift % LANES else row

    def unpack(k):
        for a in range(nl * chunks[k][1] // TILE):
            for h in range(halves_count):
                pieces = [got[a, b, h, tile(k * TILE), :] for b in range(nj)]
                for i in range(GROUP):
                    row = turned(pieces[nj - 1], LANES - cols - SLOT * i)
                    row = jnp.where(lane < LANES - 4, turned(pieces[0], lon_count - SLOT * i), row)
                    for b in reversed(range(nj)):
                        row = jnp.where(lane < cols * (b + 1), turned(pieces[b], cols * b - SLOT * i), row)
                    field[k, tile((a * rows + h * GROUP + i + 2) * TILE), :] = row
        edges(field, k)

    def edges(padded, k):
        count = chunks[k][1]
        lines = lat_count * count // TILE
        for j in range(2):
            above, below = padded[k, tile((lines + j) * TILE), :], padded[k, tile((2 + j) * TILE), :]
            blank = jnp.zeros_like(above)
            if count < TILE:
                above = jnp.where(sublane >= count, pltpu.roll(above, count, 0), blank)
                below = jnp.where(sublane < TILE - count, pltpu.roll(below, TILE - count, 0), blank)
            else:
                above = below = blank
            padded[k, tile(j * TILE), :] = above
            padded[k, tile((lines + 2 + j) * TILE), :] = below

    def stencil(source, s, k, emit):
        step_rows = TILE
        for g in range(lat_count * chunks[k][1] // TILE // step_rows):
            base = g * step_rows
            lines = [source[k, tile((base + j) * TILE), :] for j in range(step_rows + 4)]
            sums = [lines[j + 2] for j in range(step_rows)]
            for b in range(5):
                weights = [taps[s, k, a * 5 + b] for a in range(5)]
                for j in range(step_rows):
                    term = weights[0] * lines[j]
                    for a in range(1, 5):
                        term = term + weights[a] * lines[j + a]
                    sums[j] = sums[j] + turned(term, 2 - b)
            emit(g, base, sums)

    def lines_of(k, c, skip):
        count = chunks[k][1]
        lines = lat_count * count // TILE
        return [pl.ds(skip * TILE + q * count + c, lines, stride=TILE) for q in range(TILE // count)]

    def transform(k):
        count = chunks[k][1]
        by_channel = jnp.concatenate(
            [first[k, at, :] for c in range(count) for at in lines_of(k, c, 0)], axis=0
        )
        high, low = halves(by_channel)
        coeffs = lax.dot_general(
            fwd[...], jnp.concatenate([high, low, high], axis=1), (((1,), (1,)), ((), ())),
            preferred_element_type=f32,
        )
        for p in range(count // 2):
            for r in range(2):
                part = [coeffs[(2 * s + r) * pairs : (2 * s + r + 1) * pairs, lanes_of(p)] for s in range(2)]
                even = jnp.where(low_half, part[0], pltpu.roll(part[1], HALF, 1))
                odd = jnp.where(low_half, pltpu.roll(part[0], HALF, 1), part[1])
                spec_in[k, pl.ds(r * TILE + 2 * p, pairs, stride=2 * TILE), :] = even
                spec_in[k, pl.ds(r * TILE + 2 * p + 1, pairs, stride=2 * TILE), :] = odd

    def lanes_of(p):
        return slice(p * LANES, (p + 1) * LANES)

    def degrees(k):
        gain = gain_col[pl.ds(start_of(k, la), TILE), :]
        gain = jnp.concatenate([gain, gain], axis=0)
        for m in range(pairs):
            at = pl.ds(m * 2 * TILE, 2 * TILE)
            spectrum = mm_wide(spec_in[k, at, :], into[m]) * gain
            spec_out[k, at, :] = mm_wide(spectrum, onto[m])

    def synthesis(k):
        count = chunks[k][1]
        rows_of = [[None] * (count // 2) for _ in range(4)]
        for p in range(count // 2):
            for r in range(2):
                even = spec_out[k, pl.ds(r * TILE + 2 * p, pairs, stride=2 * TILE), :]
                odd = spec_out[k, pl.ds(r * TILE + 2 * p + 1, pairs, stride=2 * TILE), :]
                rows_of[r][p] = jnp.where(low_half, even, pltpu.roll(odd, HALF, 1))
                rows_of[2 + r][p] = jnp.where(low_half, pltpu.roll(even, HALF, 1), odd)
        blank = jnp.zeros((LANES - 4 * pairs, LANES), f32)
        for p in range(count // 2):
            square = jnp.concatenate([rows_of[q][p] for q in range(4)] + [blank], axis=0).T
            high, low = halves(square)
            values = mm(jnp.concatenate([high, low, high], axis=1), back[...])
            for e in range(2):
                places = list(zip(lines_of(k, 2 * p + e, 0), lines_of(k, 2 * p + e, 2)))
                lines = lat_count // len(places)
                for q, (before, after) in enumerate(places):
                    base = e * lat_count + q * lines
                    second[k, after, :] = first[k, before, :] + values[base : base + lines]
        edges(second, k)

    def emit_first(k):
        def emit(g, base, sums):
            for j, row in enumerate(sums):
                first[k, tile((base + j) * TILE), :] = row
        return emit

    def emit_second(k):
        def emit(a, base, sums):
            for h in range(halves_count):
                for b in range(nj):
                    packed = None
                    for i in reversed(range(GROUP)):
                        moved = turned(sums[h * GROUP + i], SLOT * i - cols * b)
                        packed = moved if packed is None else jnp.where(lane < SLOT * (i + 1), moved, packed)
                    back_out[a, b, h, tile(k * TILE), :] = packed
        return emit

    for k in range(len(chunks)):
        everyone(k, a_s, a_r).wait_recv()
        own_in(k).wait()
        unpack(k)
        stencil(field, 0, k, emit_first(k))
        if k == 0:
            loads[4].wait()
        transform(k)
        if k == 0:
            loads[6].wait()
            loads[7].wait()
        degrees(k)
        if k == 0:
            loads[5].wait()
        synthesis(k)
        stencil(second, 1, k, emit_second(k))
        spread(k, z_copy)
        own_back(k).start()

    loads[3].wait()
    loads[8].wait()
    loads[9].wait()
    for k in range(len(chunks)):
        everyone(k, z_s, z_r).wait_recv()
        own_back(k).wait()
    for h in range(halves_count):
        for block in range(blocks):
            parts = [home[h, b, low - b * share : high - b * share, :] for b, low, high in pieces_of(block)]
            third[pl.ds(h * LANES, LANES), lanes(block)] = jnp.concatenate(parts, axis=0).T
    state = third[...]
    average = jnp.mean(state, axis=-1, keepdims=True)
    centred = state - average
    spread = jnp.mean(centred * centred, axis=-1, keepdims=True)
    normed = (centred * lax.rsqrt(spread + 1e-05) * norm_in[...].reshape(1, channels)).astype(bf16)
    active = jax.nn.gelu(mm(normed, up[...]), approximate=True).astype(bf16)
    third[...] = state + mm(active, down[...])
    for block in range(blocks):
        for i in range(rows):
            grid[block, pl.ds(i, cols, stride=rows), :] = third[SLOT * i : SLOT * i + cols, lanes(block)]
        out_copy(block).start()
    for block in range(blocks):
        out_copy(block).wait()
    for k in range(len(chunks)):
        everyone(k, a_s, a_r).wait_send()
        everyone(k, z_s, z_r).wait_send()


def fused(nl, nj, latent, conv_first, conv_second, filter_gains, norm_gain, up_weight, down_weight):
    rows, cols, channels = latent.shape
    modes, width = filter_gains.shape
    lat_count, lon_count = rows * nl, cols * nj
    forward, back, into, onto = (jnp.asarray(t) for t in constant_tables(lat_count, lon_count, modes))
    blocks = channels // LANES
    per = channels // (nl * nj)
    count = len(chunk_list(per))
    room = count * TILE
    halves_count = rows // GROUP
    vm = lambda *shape, kind=f32: pltpu.VMEM(shape, kind)
    dma = lambda *shape: pltpu.SemaphoreType.DMA(shape)
    far = pl.BlockSpec(memory_space=pltpu.HBM)
    result = pl.pallas_call(
        functools.partial(block_kernel, nl, nj, rows, modes),
        out_shape=jax.ShapeDtypeStruct((cols * rows, channels), f32),
        in_specs=[far] * 11,
        out_specs=far,
        scratch_shapes=[
            vm(blocks, rows * SLOT, LANES),
            vm(halves_count, nj, channels // nj, LANES),
            vm(nl, nj, halves_count, room, LANES),
            vm(count, (lat_count + 4) * TILE, LANES),
            vm(count, lat_count * TILE, LANES),
            vm(count, (lat_count + 4) * TILE, LANES),
            vm(count, modes * TILE, LANES),
            vm(count, modes * TILE, LANES),
            vm(nl, nj, halves_count, room, LANES),
            vm(halves_count, nj, channels // nj, LANES),
            vm(rows * SLOT, channels),
            vm(25, channels),
            vm(25, channels),
            vm(2, channels + TILE, 32),
            vm(2, count, 25, TILE, LANES),
            vm(modes, width),
            vm(LANES, width),
            vm(width + TILE, LANES),
            vm(channels),
            vm(*forward.shape, kind=bf16),
            vm(*back.shape, kind=bf16),
            vm(*into.shape, kind=bf16),
            vm(*onto.shape, kind=bf16),
            vm(*up_weight.shape, kind=bf16),
            vm(*down_weight.shape, kind=bf16),
            dma(10), dma(blocks), dma(blocks), dma(count), dma(count),
            dma(count), dma(count), dma(count), dma(count),
        ],
        compiler_params=pltpu.CompilerParams(
            collective_id=0, has_side_effects=True, vmem_limit_bytes=60 * 1024 * 1024
        ),
        name="block",
    )(
        jnp.swapaxes(latent, 0, 1).reshape(cols * rows, channels), conv_first, conv_second,
        filter_gains, norm_gain, forward, back, into, onto, up_weight, down_weight,
    )
    return jnp.swapaxes(result.reshape(cols, rows, channels), 0, 1)


def fits(nl, nj, latent, filter_gains):
    rows, cols, channels = latent.shape
    modes = filter_gains.shape[0]
    total = nl * nj
    if rows != TILE or channels % LANES or channels % total or nj < 2 or nl < 2:
        return False
    if (channels // total) % GROUP or nl % 4 or rows * nl != HALF or cols > SLOT or cols * nj > LANES - 8 or cols < 4:
        return False
    return modes % 16 == 0 and modes <= HALF and 2 * modes <= LANES


def body(latent, conv_first, conv_second, filter_gains, norm_gain, up_weight, down_weight):
    nl, nj = lax.axis_size("lat"), lax.axis_size("lon")
    arguments = (latent, conv_first, conv_second, filter_gains, norm_gain, up_weight, down_weight)
    if fits(nl, nj, latent, filter_gains):
        return fused(nl, nj, *arguments)
    return per_device(*arguments)


def solution(mesh):
    return jax.shard_map(
        body,
        mesh=mesh,
        in_specs=(P("lat", "lon", None), P(), P(), P(None, "lon"), P(), P(), P()),
        out_specs=P("lat", "lon", None),
        check_vma=False,
    )
```

```python
import functools
import math

import jax
import jax.numpy as jnp
import numpy as np
from jax import lax
from jax.experimental import pallas as pl
from jax.experimental.pallas import tpu as pltpu
from jax.sharding import PartitionSpec as P

highest = lax.Precision.HIGHEST


def padded_2(block, sides, width):
    for axis, dim in sides:
        count = lax.axis_size(axis)
        forward = [(i, i + 1) for i in range(count - 1)]
        backward = [(target, source) for source, target in forward]
        low = lax.ppermute(
            lax.slice_in_dim(block, block.shape[dim] - width, None, axis=dim), axis, forward
        )
        high = lax.ppermute(lax.slice_in_dim(block, 0, width, axis=dim), axis, backward)
        block = jnp.concatenate([low, block, high], axis=dim)
    return block


def stencil_sum(padded, weights, row_count, col_count):
    stencil_total = jnp.zeros((row_count, col_count, padded.shape[2]), padded.dtype)
    for row_shift in range(5):
        for col_shift in range(5):
            stencil_total = (
                stencil_total
                + weights[row_shift * 5 + col_shift]
                * padded[row_shift : row_shift + row_count, col_shift : col_shift + col_count, :]
            )
    return stencil_total


def slice_stencil(sliced, weights):
    lat_extended = padded_2(sliced, (("lat", 0),), 2)
    wrapped = jnp.concatenate([lat_extended[:, -2:], lat_extended, lat_extended[:, :2]], axis=1)
    return stencil_sum(wrapped, weights, sliced.shape[0], sliced.shape[1])


def colatitude(cell_count, float_type):
    cell_index = jnp.arange(cell_count).astype(float_type)
    return jnp.pi * (cell_index + 0.5) / cell_count


def legendre_table(orders, degrees, cosine, sine_theta):
    log_seed = 0.5 * (
        jnp.log((2.0 * orders + 1.0) / (4.0 * jnp.pi))
        + jax.scipy.special.gammaln(2.0 * orders + 1.0)
        - 2.0 * orders * jnp.log(2.0)
        - 2.0 * jax.scipy.special.gammaln(orders + 1.0)
    )
    diagonal_term = jnp.exp(log_seed[:, None] + orders[:, None] * jnp.log(sine_theta)[None, :])
    blanks = jnp.zeros_like(diagonal_term)
    legendre = jnp.zeros((orders.shape[0], degrees, sine_theta.shape[0]), diagonal_term.dtype)

    def block_step(block_index, state_tuple):
        previous, earlier, legendre = state_tuple
        values = []
        for offset in range(8):
            degree = (block_index * 8 + offset).astype(diagonal_term.dtype)
            square = degree * degree
            upper_ratio = jnp.sqrt(
                jnp.maximum(4.0 * square - 1.0, 1.0) / jnp.maximum(square - orders * orders, 1.0)
            )
            below_sq = (degree - 1.0) * (degree - 1.0)
            lower_ratio = jnp.sqrt(
                jnp.maximum(below_sq - orders * orders, 0.0)
                / jnp.maximum(4.0 * below_sq - 1.0, 1.0)
            )
            recurred = upper_ratio[:, None] * (
                cosine[None, :] * previous - lower_ratio[:, None] * earlier
            )
            current = jnp.where(
                (degree < orders)[:, None],
                blanks,
                jnp.where((degree == orders)[:, None], diagonal_term, recurred),
            )
            values.append(current)
            earlier = previous
            previous = current
        stacked = jnp.stack(values, axis=1)
        legendre = lax.dynamic_update_slice(
            legendre, stacked, (jnp.int32(0), (block_index * 8).astype(jnp.int32), jnp.int32(0))
        )
        return (previous, earlier, legendre)

    return lax.fori_loop(0, degrees // 8, block_step, (blanks, blanks, legendre))[2]


def fourier_tables(lon_count, mode_count, float_type):
    product_index = jnp.arange(lon_count)[:, None] * jnp.arange(mode_count)[None, :] % lon_count
    phase_grid = 2.0 * jnp.pi * product_index.astype(float_type) / lon_count
    forward = jnp.stack([jnp.cos(phase_grid), -jnp.sin(phase_grid)], axis=1) / lon_count
    factor = jnp.where(jnp.arange(mode_count) == 0, 1.0, 2.0).astype(float_type)
    inverse = jnp.stack(
        [jnp.cos(phase_grid).T * factor[:, None], -jnp.sin(phase_grid).T * factor[:, None]], axis=0
    )
    return (forward, inverse)


def channel_mlp(latent, norm_gain, up_weight, down_weight):
    average = jnp.mean(latent, axis=-1, keepdims=True)
    centred = latent - average
    spread = jnp.mean(centred * centred, axis=-1, keepdims=True)
    normed = (centred * lax.rsqrt(spread + 1e-05) * norm_gain).astype(jnp.bfloat16)
    hidden = jnp.dot(normed, up_weight, preferred_element_type=jnp.float32)
    active = jax.nn.gelu(hidden, approximate=True).astype(jnp.bfloat16)
    return latent + jnp.dot(active, down_weight, preferred_element_type=jnp.float32)


def per_device(latent, conv_first, conv_second, filter_gains, norm_gain, up_weight, down_weight):
    lat_size = lax.axis_size("lat")
    lon_size = lax.axis_size("lon")
    lat_local = latent.shape[0]
    lon_local = latent.shape[1]
    slice_width = filter_gains.shape[1]
    mode_count = filter_gains.shape[0]
    lat_count = lat_local * lat_size
    lon_count = lon_local * lon_size
    order_count = mode_count // lat_size
    channel_start = lax.axis_index("lon") * slice_width
    sliced = lax.all_to_all(latent, "lon", split_axis=2, concat_axis=1, tiled=True)
    first_taps = lax.dynamic_slice_in_dim(conv_first, channel_start, slice_width, 1)
    first_sliced = sliced + slice_stencil(sliced, first_taps)
    forward, inverse = fourier_tables(lon_count, mode_count, jnp.float32)
    colat_grid = colatitude(lat_count, jnp.float32)
    orders = (lax.axis_index("lat") * order_count + jnp.arange(order_count)).astype(jnp.float32)
    legendre = legendre_table(orders, mode_count, jnp.cos(colat_grid), jnp.sin(colat_grid))
    quadrature = 2.0 * jnp.pi * jnp.pi * jnp.sin(colat_grid) / lat_count
    weighted = legendre * quadrature
    coeffs = jnp.einsum("inc,nrk->irkc", first_sliced, forward, precision=highest)
    spectrum = jnp.einsum(
        "kli,irkc->lrkc",
        weighted,
        lax.all_to_all(coeffs, "lat", split_axis=2, concat_axis=0, tiled=True),
        precision=highest,
    )
    spectrum = spectrum * filter_gains[:, None, None, :]
    restored = jnp.einsum("kli,lrkc->irkc", legendre, spectrum, precision=highest)
    returned = lax.all_to_all(restored, "lat", split_axis=0, concat_axis=2, tiled=True)
    filtered = jnp.einsum("irkc,rkn->inc", returned, inverse, precision=highest)
    second_taps = lax.dynamic_slice_in_dim(conv_second, channel_start, slice_width, 1)
    second_sliced = first_sliced + filtered
    incoming = second_sliced + slice_stencil(second_sliced, second_taps)
    arrived = lax.all_to_all(incoming, "lon", split_axis=1, concat_axis=2, tiled=True)
    return channel_mlp(arrived, norm_gain, up_weight, down_weight)


LANES = 128
TILE = 8
GROUP = 4
SLOT = LANES // GROUP
HALF = LANES // 2
bf16 = jnp.bfloat16
f32 = jnp.float32


def legendre_numpy(modes, lat_count):
    theta = np.pi * (np.arange(lat_count) + 0.5) / lat_count
    cosine, sine = np.cos(theta), np.sin(theta)
    table = np.zeros((modes, modes, lat_count))
    for m in range(modes):
        seed = 0.5 * (
            math.log((2 * m + 1) / (4 * math.pi))
            + math.lgamma(2 * m + 1)
            - 2 * m * math.log(2.0)
            - 2 * math.lgamma(m + 1)
        )
        table[m, m] = np.exp(seed + m * np.log(sine))
        for l in range(m + 1, modes):
            a = math.sqrt((4.0 * l * l - 1) / (l * l - m * m))
            b = math.sqrt(max((l - 1.0) ** 2 - m * m, 0.0) / (4.0 * (l - 1.0) ** 2 - 1)) if l > 1 else 0.0
            earlier = table[m, l - 2] if l > m + 1 else 0.0
            table[m, l] = a * (cosine * table[m, l - 1] - b * earlier)
    quadrature = 2 * np.pi**2 * sine / lat_count
    return table, table * quadrature


def split_numpy(table):
    high = table.astype(np.float32).astype(jnp.bfloat16)
    low = (table - high.astype(np.float64)).astype(np.float32).astype(jnp.bfloat16)
    return high, low


@functools.lru_cache(maxsize=None)
def constant_tables(lat_count, lon_count, modes):
    pairs = modes // 2
    n = np.arange(lon_count)
    k = np.arange(modes)
    phase = 2 * np.pi * ((k[:, None] * n[None, :]) % lon_count) / lon_count
    trig = np.stack([np.cos(phase), -np.sin(phase)], axis=1)
    by_row = trig.reshape(2, pairs, 2, lon_count).transpose(0, 2, 1, 3).reshape(2 * modes, lon_count)
    forward = np.zeros((2 * modes, LANES))
    forward[:, :lon_count] = by_row / lon_count
    high, low = split_numpy(forward)
    forward = np.concatenate([high, high, low], axis=1)
    factor = np.where(k == 0, 1.0, 2.0)
    scaled = (trig * factor[:, None, None]).reshape(2, pairs, 2, lon_count).transpose(0, 2, 1, 3)
    scaled = scaled.reshape(2 * modes, lon_count)
    back = np.zeros((LANES, LANES))
    back[: 2 * modes, :lon_count] = scaled
    back[: 2 * modes, lon_count : lon_count + 2] = scaled[:, :2]
    back[: 2 * modes, LANES - 2 :] = scaled[:, lon_count - 2 :]
    high, low = split_numpy(back)
    back = np.concatenate([high, high, low], axis=0)
    table, weighted = legendre_numpy(modes, lat_count)
    into = np.zeros((pairs, LANES, LANES))
    onto = np.zeros((pairs, LANES, LANES))
    for s in range(2):
        part = slice(s * pairs, (s + 1) * pairs)
        lat, deg = slice(s * HALF, s * HALF + lat_count), slice(s * HALF, s * HALF + modes)
        into[:, lat, deg] = np.swapaxes(weighted[part], 1, 2)
        onto[:, deg, lat] = table[part]
    into = np.concatenate(split_numpy(into), axis=2)
    onto = np.concatenate(split_numpy(onto), axis=2)
    return forward, back, into, onto


def halves(value):
    high = value.astype(bf16)
    return high, (value - high.astype(f32)).astype(bf16)


def mm(a, b):
    return jnp.dot(a, b, preferred_element_type=f32)


def mm_wide(value, table):
    count = value.shape[0]
    high, low = halves(value)
    out = mm(jnp.concatenate([high, low], axis=0), table)
    return (out[:count, :LANES] + out[count:, :LANES]) + (out[:count, LANES:] + out[count:, LANES:])


def chunk_list(per):
    chunks = [(start, TILE) for start in range(0, per - per % TILE, TILE)]
    if per % TILE:
        chunks.append((per - per % TILE, per % TILE))
    return chunks


def block_kernel(
    nl, nj, rows, modes,
    latent, conv_first, conv_second, gains, norm_gain, fwd_hbm, back_hbm, into_hbm, onto_hbm, up_hbm, down_hbm,
    out,
    grid, sent, got, field, first, second, spec_in, spec_out, back_out, home, third,
    tap_one, tap_two, tap_col, taps, gain_in, gain_wide, gain_col, norm_in, fwd, back, into, onto, up, down,
    load_sem, in_sem, own_a, own_z, a_s, a_r, z_s, z_r,
):
    channels = latent.shape[1]
    cols = latent.shape[0] // rows
    blocks = channels // LANES
    total = nl * nj
    per = channels // total
    chunks = chunk_list(per)
    halves_count = rows // GROUP
    lat_count = rows * nl
    lon_count = cols * nj
    pairs = modes // 2
    la, lo = lax.axis_index("lat"), lax.axis_index("lon")
    me = lo * nl + la

    share = nl * per
    z_at, core = la // 2, lax.rem(la, 2)
    across = nl // 2

    def pieces_of(block):
        out, low = [], block * LANES
        while low < (block + 1) * LANES:
            high = min((block + 1) * LANES, (low // share + 1) * share)
            out.append((low // share, low, high))
            low = high
        return out

    def start_of(k, a):
        start, count = chunks[k]
        if per % TILE == 0:
            return a * per + start
        odd = lax.rem(a, 2)
        if count == TILE:
            return pl.multiple_of(a * per + odd * (per % TILE) + start, TILE)
        return a * per + (1 - odd) * start

    def channels_of(k, a, b):
        return (slice(None), b, pl.ds(start_of(k, a), chunks[k][1]), slice(None))

    def place_of(k, a, b):
        count = chunks[k][1]
        bands = nl * count // TILE
        return (lax.rem(a, bands), b, slice(None), pl.ds(k * TILE + a // bands * count, count), slice(None))

    def lanes(block):
        return pl.ds(block * LANES, LANES)

    def tile(start):
        return pl.ds(start if isinstance(start, int) else pl.multiple_of(start, TILE), TILE)

    def rcopy(src, dst, send, recv, a, b):
        return pltpu.make_async_remote_copy(
            src_ref=src, dst_ref=dst, send_sem=send, recv_sem=recv,
            device_id={"lat": a, "lon": b}, device_id_type=pl.DeviceIdType.MESH,
        )

    def others(action):
        for d in range(1, nj):
            action(la, lax.rem(lo + d, nj))

        def step(d, carry):
            a = lax.rem(la + d, nl)
            for b in range(nj):
                action(a, lax.rem(lo + b, nj))
            return carry

        lax.fori_loop(1, nl, step, 0)

    barrier = pltpu.get_barrier_semaphore()
    others(
        lambda a, b: pl.semaphore_signal(
            barrier, inc=1, device_id={"lat": a, "lon": b}, device_id_type=pl.DeviceIdType.MESH
        )
    )

    pairs_of = (
        (conv_first, tap_one), (conv_second, tap_two), (gains, gain_in),
        (norm_gain, norm_in), (fwd_hbm, fwd), (back_hbm, back), (into_hbm, into), (onto_hbm, onto),
        (up_hbm, up), (down_hbm, down),
    )
    loads = [pltpu.make_async_copy(a, b, load_sem.at[i]) for i, (a, b) in enumerate(pairs_of)]

    def in_copy(block):
        return pltpu.make_async_copy(
            latent.at[:, lanes(block)], grid.at[block, pl.ds(0, rows * cols)], in_sem.at[block]
        )

    for block in range(blocks):
        in_copy(block).start()

    for block in range(blocks):
        grid[block, rows * cols :, :] = jnp.zeros((rows * (SLOT - cols), LANES), f32)

    for block in range(blocks):
        in_copy(block).wait()
        if block + 1 == blocks:
            for load in loads:
                load.start()
        for h in range(halves_count):
            parts = [grid[block, pl.ds(h * GROUP + i, SLOT, stride=rows), :] for i in range(GROUP)]
            block_rows = jnp.concatenate(parts, axis=0).T
            for b, low, high in pieces_of(block):
                sent[h, b, low - b * share : high - b * share, :] = block_rows[low - block * LANES : high - block * LANES]

    def a_copy(k, a, b):
        return rcopy(sent.at[channels_of(k, a, b)], got.at[place_of(k, la, lo)], a_s.at[k], a_r.at[k], a, b)

    def z_copy(k, a, b):
        return rcopy(back_out.at[place_of(k, a, b)], home.at[channels_of(k, la, lo)], z_s.at[k], z_r.at[k], a, b)

    def own_in(k):
        return pltpu.make_async_copy(sent.at[channels_of(k, la, lo)], got.at[place_of(k, la, lo)], own_a.at[k])

    def own_back(k):
        return pltpu.make_async_copy(back_out.at[place_of(k, la, lo)], home.at[channels_of(k, la, lo)], own_z.at[k])

    def everyone(k, send, recv):
        whole = first.at[0, pl.ds(0, (total - 1) * halves_count * chunks[k][1])]
        return rcopy(whole, whole, send.at[k], recv.at[k], lax.rem(la + 1, nl), lo)

    def spread(k, copy):
        def band(d, flip, start):
            a = lax.rem(z_at + d, across) * 2 + (1 - core if flip else core)
            for b in range(start, nj):
                copy(k, a, lax.rem(lo + b, nj)).start()

        for d in [0] + [e for q in range(1, across // 2 + 1) for e in sorted({q, across - q})]:
            band(d, False, 1 if d == 0 else 0)
            band(d, True, 0)

    pl.semaphore_wait(barrier, total - 1)
    def send_in(k):
        spread(k, a_copy)
        own_in(k).start()

    for k in range(len(chunks)):
        send_in(k)

    loads[0].wait()
    loads[1].wait()
    loads[2].wait()
    gain_wide[...] = jnp.zeros_like(gain_wide)
    gain_wide[0:modes, :] = gain_in[...]
    gain_wide[HALF : HALF + modes, :] = gain_in[...]
    width = gain_in.shape[1]
    for start in range(0, width, LANES):
        stop = min(start + LANES, width)
        gain_col[start:stop, :] = gain_wide[:, start:stop].T
    for s, source in enumerate((tap_one, tap_two)):
        for block in range(blocks):
            square = jnp.concatenate([source[:, lanes(block)], jnp.zeros((7, LANES), f32)], axis=0)
            tap_col[s, lanes(block), :] = square.T
        for k, (_, count) in enumerate(chunks):
            own = tap_col[s, pl.ds(lo * share + start_of(k, la), TILE), :]
            if count < TILE:
                own = jnp.concatenate([own[:count]] * (TILE // count), axis=0)
            for t in range(25):
                taps[s, k, t] = jnp.broadcast_to(own[:, t : t + 1], (TILE, LANES))

    lane = lax.broadcasted_iota(jnp.int32, (TILE, LANES), 1)
    sublane = lax.broadcasted_iota(jnp.int32, (TILE, LANES), 0)
    low_half = lax.broadcasted_iota(jnp.int32, (pairs, LANES), 1) < HALF

    def turned(row, shift):
        return pltpu.roll(row, shift % LANES, 1) if shift % LANES else row

    def unpack(k):
        for a in range(nl * chunks[k][1] // TILE):
            for h in range(halves_count):
                pieces = [got[a, b, h, tile(k * TILE), :] for b in range(nj)]
                for i in range(GROUP):
                    row = turned(pieces[nj - 1], LANES - cols - SLOT * i)
                    row = jnp.where(lane < LANES - 4, turned(pieces[0], lon_count - SLOT * i), row)
                    for b in reversed(range(nj)):
                        row = jnp.where(lane < cols * (b + 1), turned(pieces[b], cols * b - SLOT * i), row)
                    field[k, tile((a * rows + h * GROUP + i + 2) * TILE), :] = row
        edges(field, k)

    def edges(padded, k):
        count = chunks[k][1]
        lines = lat_count * count // TILE
        for j in range(2):
            above, below = padded[k, tile((lines + j) * TILE), :], padded[k, tile((2 + j) * TILE), :]
            blank = jnp.zeros_like(above)
            if count < TILE:
                above = jnp.where(sublane >= count, pltpu.roll(above, count, 0), blank)
                below = jnp.where(sublane < TILE - count, pltpu.roll(below, TILE - count, 0), blank)
            else:
                above = below = blank
            padded[k, tile(j * TILE), :] = above
            padded[k, tile((lines + 2 + j) * TILE), :] = below

    def stencil(source, s, k, emit):
        step_rows = TILE
        for g in range(lat_count * chunks[k][1] // TILE // step_rows):
            base = g * step_rows
            lines = [source[k, tile((base + j) * TILE), :] for j in range(step_rows + 4)]
            sums = [lines[j + 2] for j in range(step_rows)]
            for b in range(5):
                weights = [taps[s, k, a * 5 + b] for a in range(5)]
                for j in range(step_rows):
                    term = weights[0] * lines[j]
                    for a in range(1, 5):
                        term = term + weights[a] * lines[j + a]
                    sums[j] = sums[j] + turned(term, 2 - b)
            emit(g, base, sums)

    def lines_of(k, c, skip):
        count = chunks[k][1]
        lines = lat_count * count // TILE
        return [pl.ds(skip * TILE + q * count + c, lines, stride=TILE) for q in range(TILE // count)]

    def transform(k):
        count = chunks[k][1]
        by_channel = jnp.concatenate(
            [first[k, at, :] for c in range(count) for at in lines_of(k, c, 0)], axis=0
        )
        high, low = halves(by_channel)
        coeffs = lax.dot_general(
            fwd[...], jnp.concatenate([high, low, high], axis=1), (((1,), (1,)), ((), ())),
            preferred_element_type=f32,
        )
        for p in range(count // 2):
            for r in range(2):
                part = [coeffs[(2 * s + r) * pairs : (2 * s + r + 1) * pairs, lanes_of(p)] for s in range(2)]
                even = jnp.where(low_half, part[0], pltpu.roll(part[1], HALF, 1))
                odd = jnp.where(low_half, pltpu.roll(part[0], HALF, 1), part[1])
                spec_in[k, pl.ds(r * TILE + 2 * p, pairs, stride=2 * TILE), :] = even
                spec_in[k, pl.ds(r * TILE + 2 * p + 1, pairs, stride=2 * TILE), :] = odd

    def lanes_of(p):
        return slice(p * LANES, (p + 1) * LANES)

    def degrees(k):
        gain = gain_col[pl.ds(start_of(k, la), TILE), :]
        gain = jnp.concatenate([gain, gain], axis=0)
        for m in range(pairs):
            at = pl.ds(m * 2 * TILE, 2 * TILE)
            spectrum = mm_wide(spec_in[k, at, :], into[m]) * gain
            spec_out[k, at, :] = mm_wide(spectrum, onto[m])

    def synthesis(k):
        count = chunks[k][1]
        rows_of = [[None] * (count // 2) for _ in range(4)]
        for p in range(count // 2):
            for r in range(2):
                even = spec_out[k, pl.ds(r * TILE + 2 * p, pairs, stride=2 * TILE), :]
                odd = spec_out[k, pl.ds(r * TILE + 2 * p + 1, pairs, stride=2 * TILE), :]
                rows_of[r][p] = jnp.where(low_half, even, pltpu.roll(odd, HALF, 1))
                rows_of[2 + r][p] = jnp.where(low_half, pltpu.roll(even, HALF, 1), odd)
        blank = jnp.zeros((LANES - 4 * pairs, LANES), f32)
        for p in range(count // 2):
            square = jnp.concatenate([rows_of[q][p] for q in range(4)] + [blank], axis=0).T
            high, low = halves(square)
            values = mm(jnp.concatenate([high, low, high], axis=1), back[...])
            for e in range(2):
                places = list(zip(lines_of(k, 2 * p + e, 0), lines_of(k, 2 * p + e, 2)))
                lines = lat_count // len(places)
                for q, (before, after) in enumerate(places):
                    base = e * lat_count + q * lines
                    second[k, after, :] = first[k, before, :] + values[base : base + lines]
        edges(second, k)

    def emit_first(k):
        def emit(g, base, sums):
            for j, row in enumerate(sums):
                first[k, tile((base + j) * TILE), :] = row
        return emit

    def emit_second(k):
        def emit(a, base, sums):
            for h in range(halves_count):
                for b in range(nj):
                    packed = None
                    for i in reversed(range(GROUP)):
                        moved = turned(sums[h * GROUP + i], SLOT * i - cols * b)
                        packed = moved if packed is None else jnp.where(lane < SLOT * (i + 1), moved, packed)
                    back_out[a, b, h, tile(k * TILE), :] = packed
        return emit

    for k in range(len(chunks)):
        everyone(k, a_s, a_r).wait_recv()
        own_in(k).wait()
        unpack(k)
        stencil(field, 0, k, emit_first(k))
        if k == 0:
            loads[4].wait()
        transform(k)
        if k == 0:
            loads[6].wait()
            loads[7].wait()
        degrees(k)
        if k == 0:
            loads[5].wait()
        synthesis(k)
        stencil(second, 1, k, emit_second(k))
        spread(k, z_copy)
        own_back(k).start()

    loads[3].wait()
    loads[8].wait()
    loads[9].wait()
    for k in range(len(chunks)):
        everyone(k, z_s, z_r).wait_recv()
        own_back(k).wait()
    for h in range(halves_count):
        for block in range(blocks):
            parts = [home[h, b, low - b * share : high - b * share, :] for b, low, high in pieces_of(block)]
            third[pl.ds(h * LANES, LANES), lanes(block)] = jnp.concatenate(parts, axis=0).T
    state = third[...]
    average = jnp.mean(state, axis=-1, keepdims=True)
    centred = state - average
    spread = jnp.mean(centred * centred, axis=-1, keepdims=True)
    normed = (centred * lax.rsqrt(spread + 1e-05) * norm_in[...].reshape(1, channels)).astype(bf16)
    active = jax.nn.gelu(mm(normed, up[...]), approximate=True).astype(bf16)
    result = state + mm(active, down[...])
    for block in range(blocks):
        for i in range(rows):
            grid[block, pl.ds(i, cols, stride=rows), :] = (
                result[SLOT * i : SLOT * i + cols, block * LANES : (block + 1) * LANES]
            )
        out[:, lanes(block)] = grid[block, 0 : rows * cols, :]
    for k in range(len(chunks)):
        everyone(k, a_s, a_r).wait_send()
        everyone(k, z_s, z_r).wait_send()


def fused(nl, nj, latent, conv_first, conv_second, filter_gains, norm_gain, up_weight, down_weight):
    rows, cols, channels = latent.shape
    modes, width = filter_gains.shape
    lat_count, lon_count = rows * nl, cols * nj
    forward, back, into, onto = (jnp.asarray(t) for t in constant_tables(lat_count, lon_count, modes))
    blocks = channels // LANES
    per = channels // (nl * nj)
    count = len(chunk_list(per))
    room = count * TILE
    halves_count = rows // GROUP
    vm = lambda *shape, kind=f32: pltpu.VMEM(shape, kind)
    dma = lambda *shape: pltpu.SemaphoreType.DMA(shape)
    far = pl.BlockSpec(memory_space=pltpu.HBM)
    result = pl.pallas_call(
        functools.partial(block_kernel, nl, nj, rows, modes),
        out_shape=pltpu.VMEM((cols * rows, channels), f32),
        in_specs=[far] * 11,
        out_specs=pl.BlockSpec(memory_space=pltpu.VMEM),
        scratch_shapes=[
            vm(blocks, rows * SLOT, LANES),
            vm(halves_count, nj, channels // nj, LANES),
            vm(nl, nj, halves_count, room, LANES),
            vm(count, (lat_count + 4) * TILE, LANES),
            vm(count, lat_count * TILE, LANES),
            vm(count, (lat_count + 4) * TILE, LANES),
            vm(count, modes * TILE, LANES),
            vm(count, modes * TILE, LANES),
            vm(nl, nj, halves_count, room, LANES),
            vm(halves_count, nj, channels // nj, LANES),
            vm(rows * SLOT, channels),
            vm(25, channels),
            vm(25, channels),
            vm(2, channels + TILE, 32),
            vm(2, count, 25, TILE, LANES),
            vm(modes, width),
            vm(LANES, width),
            vm(width + TILE, LANES),
            vm(channels),
            vm(*forward.shape, kind=bf16),
            vm(*back.shape, kind=bf16),
            vm(*into.shape, kind=bf16),
            vm(*onto.shape, kind=bf16),
            vm(*up_weight.shape, kind=bf16),
            vm(*down_weight.shape, kind=bf16),
            dma(10), dma(blocks), dma(count), dma(count),
            dma(count), dma(count), dma(count), dma(count),
        ],
        compiler_params=pltpu.CompilerParams(
            collective_id=0, has_side_effects=True, vmem_limit_bytes=60 * 1024 * 1024
        ),
        name="block",
    )(
        jnp.swapaxes(latent, 0, 1).reshape(cols * rows, channels), conv_first, conv_second,
        filter_gains, norm_gain, forward, back, into, onto, up_weight, down_weight,
    )
    return jnp.swapaxes(result.reshape(cols, rows, channels), 0, 1)


def fits(nl, nj, latent, filter_gains):
    rows, cols, channels = latent.shape
    modes = filter_gains.shape[0]
    total = nl * nj
    if rows != TILE or channels % LANES or channels % total or nj < 2 or nl < 2:
        return False
    if (channels // total) % GROUP or nl % 4 or rows * nl != HALF or cols > SLOT or cols * nj > LANES - 8 or cols < 4:
        return False
    return modes % 16 == 0 and modes <= HALF and 2 * modes <= LANES


def body(latent, conv_first, conv_second, filter_gains, norm_gain, up_weight, down_weight):
    nl, nj = lax.axis_size("lat"), lax.axis_size("lon")
    arguments = (latent, conv_first, conv_second, filter_gains, norm_gain, up_weight, down_weight)
    if fits(nl, nj, latent, filter_gains):
        return fused(nl, nj, *arguments)
    return per_device(*arguments)


def solution(mesh):
    return jax.shard_map(
        body,
        mesh=mesh,
        in_specs=(P("lat", "lon", None), P(), P(), P(None, "lon"), P(), P(), P()),
        out_specs=P("lat", "lon", None),
        check_vma=False,
    )
```

```python
import functools
import math

import jax
import jax.numpy as jnp
import numpy as np
from jax import lax
from jax.experimental import pallas as pl
from jax.experimental.pallas import tpu as pltpu
from jax.sharding import PartitionSpec as P

highest = lax.Precision.HIGHEST


def padded_2(block, sides, width):
    for axis, dim in sides:
        count = lax.axis_size(axis)
        forward = [(i, i + 1) for i in range(count - 1)]
        backward = [(target, source) for source, target in forward]
        low = lax.ppermute(
            lax.slice_in_dim(block, block.shape[dim] - width, None, axis=dim), axis, forward
        )
        high = lax.ppermute(lax.slice_in_dim(block, 0, width, axis=dim), axis, backward)
        block = jnp.concatenate([low, block, high], axis=dim)
    return block


def stencil_sum(padded, weights, row_count, col_count):
    stencil_total = jnp.zeros((row_count, col_count, padded.shape[2]), padded.dtype)
    for row_shift in range(5):
        for col_shift in range(5):
            stencil_total = (
                stencil_total
                + weights[row_shift * 5 + col_shift]
                * padded[row_shift : row_shift + row_count, col_shift : col_shift + col_count, :]
            )
    return stencil_total


def slice_stencil(sliced, weights):
    lat_extended = padded_2(sliced, (("lat", 0),), 2)
    wrapped = jnp.concatenate([lat_extended[:, -2:], lat_extended, lat_extended[:, :2]], axis=1)
    return stencil_sum(wrapped, weights, sliced.shape[0], sliced.shape[1])


def colatitude(cell_count, float_type):
    cell_index = jnp.arange(cell_count).astype(float_type)
    return jnp.pi * (cell_index + 0.5) / cell_count


def legendre_table(orders, degrees, cosine, sine_theta):
    log_seed = 0.5 * (
        jnp.log((2.0 * orders + 1.0) / (4.0 * jnp.pi))
        + jax.scipy.special.gammaln(2.0 * orders + 1.0)
        - 2.0 * orders * jnp.log(2.0)
        - 2.0 * jax.scipy.special.gammaln(orders + 1.0)
    )
    diagonal_term = jnp.exp(log_seed[:, None] + orders[:, None] * jnp.log(sine_theta)[None, :])
    blanks = jnp.zeros_like(diagonal_term)
    legendre = jnp.zeros((orders.shape[0], degrees, sine_theta.shape[0]), diagonal_term.dtype)

    def block_step(block_index, state_tuple):
        previous, earlier, legendre = state_tuple
        values = []
        for offset in range(8):
            degree = (block_index * 8 + offset).astype(diagonal_term.dtype)
            square = degree * degree
            upper_ratio = jnp.sqrt(
                jnp.maximum(4.0 * square - 1.0, 1.0) / jnp.maximum(square - orders * orders, 1.0)
            )
            below_sq = (degree - 1.0) * (degree - 1.0)
            lower_ratio = jnp.sqrt(
                jnp.maximum(below_sq - orders * orders, 0.0)
                / jnp.maximum(4.0 * below_sq - 1.0, 1.0)
            )
            recurred = upper_ratio[:, None] * (
                cosine[None, :] * previous - lower_ratio[:, None] * earlier
            )
            current = jnp.where(
                (degree < orders)[:, None],
                blanks,
                jnp.where((degree == orders)[:, None], diagonal_term, recurred),
            )
            values.append(current)
            earlier = previous
            previous = current
        stacked = jnp.stack(values, axis=1)
        legendre = lax.dynamic_update_slice(
            legendre, stacked, (jnp.int32(0), (block_index * 8).astype(jnp.int32), jnp.int32(0))
        )
        return (previous, earlier, legendre)

    return lax.fori_loop(0, degrees // 8, block_step, (blanks, blanks, legendre))[2]


def fourier_tables(lon_count, mode_count, float_type):
    product_index = jnp.arange(lon_count)[:, None] * jnp.arange(mode_count)[None, :] % lon_count
    phase_grid = 2.0 * jnp.pi * product_index.astype(float_type) / lon_count
    forward = jnp.stack([jnp.cos(phase_grid), -jnp.sin(phase_grid)], axis=1) / lon_count
    factor = jnp.where(jnp.arange(mode_count) == 0, 1.0, 2.0).astype(float_type)
    inverse = jnp.stack(
        [jnp.cos(phase_grid).T * factor[:, None], -jnp.sin(phase_grid).T * factor[:, None]], axis=0
    )
    return (forward, inverse)


def channel_mlp(latent, norm_gain, up_weight, down_weight):
    average = jnp.mean(latent, axis=-1, keepdims=True)
    centred = latent - average
    spread = jnp.mean(centred * centred, axis=-1, keepdims=True)
    normed = (centred * lax.rsqrt(spread + 1e-05) * norm_gain).astype(jnp.bfloat16)
    hidden = jnp.dot(normed, up_weight, preferred_element_type=jnp.float32)
    active = jax.nn.gelu(hidden, approximate=True).astype(jnp.bfloat16)
    return latent + jnp.dot(active, down_weight, preferred_element_type=jnp.float32)


def per_device(latent, conv_first, conv_second, filter_gains, norm_gain, up_weight, down_weight):
    lat_size = lax.axis_size("lat")
    lon_size = lax.axis_size("lon")
    lat_local = latent.shape[0]
    lon_local = latent.shape[1]
    slice_width = filter_gains.shape[1]
    mode_count = filter_gains.shape[0]
    lat_count = lat_local * lat_size
    lon_count = lon_local * lon_size
    order_count = mode_count // lat_size
    channel_start = lax.axis_index("lon") * slice_width
    sliced = lax.all_to_all(latent, "lon", split_axis=2, concat_axis=1, tiled=True)
    first_taps = lax.dynamic_slice_in_dim(conv_first, channel_start, slice_width, 1)
    first_sliced = sliced + slice_stencil(sliced, first_taps)
    forward, inverse = fourier_tables(lon_count, mode_count, jnp.float32)
    colat_grid = colatitude(lat_count, jnp.float32)
    orders = (lax.axis_index("lat") * order_count + jnp.arange(order_count)).astype(jnp.float32)
    legendre = legendre_table(orders, mode_count, jnp.cos(colat_grid), jnp.sin(colat_grid))
    quadrature = 2.0 * jnp.pi * jnp.pi * jnp.sin(colat_grid) / lat_count
    weighted = legendre * quadrature
    coeffs = jnp.einsum("inc,nrk->irkc", first_sliced, forward, precision=highest)
    spectrum = jnp.einsum(
        "kli,irkc->lrkc",
        weighted,
        lax.all_to_all(coeffs, "lat", split_axis=2, concat_axis=0, tiled=True),
        precision=highest,
    )
    spectrum = spectrum * filter_gains[:, None, None, :]
    restored = jnp.einsum("kli,lrkc->irkc", legendre, spectrum, precision=highest)
    returned = lax.all_to_all(restored, "lat", split_axis=0, concat_axis=2, tiled=True)
    filtered = jnp.einsum("irkc,rkn->inc", returned, inverse, precision=highest)
    second_taps = lax.dynamic_slice_in_dim(conv_second, channel_start, slice_width, 1)
    second_sliced = first_sliced + filtered
    incoming = second_sliced + slice_stencil(second_sliced, second_taps)
    arrived = lax.all_to_all(incoming, "lon", split_axis=1, concat_axis=2, tiled=True)
    return channel_mlp(arrived, norm_gain, up_weight, down_weight)


LANES = 128
TILE = 8
GROUP = 4
SLOT = LANES // GROUP
HALF = LANES // 2
bf16 = jnp.bfloat16
f32 = jnp.float32


def legendre_numpy(modes, lat_count):
    theta = np.pi * (np.arange(lat_count) + 0.5) / lat_count
    cosine, sine = np.cos(theta), np.sin(theta)
    table = np.zeros((modes, modes, lat_count))
    for m in range(modes):
        seed = 0.5 * (
            math.log((2 * m + 1) / (4 * math.pi))
            + math.lgamma(2 * m + 1)
            - 2 * m * math.log(2.0)
            - 2 * math.lgamma(m + 1)
        )
        table[m, m] = np.exp(seed + m * np.log(sine))
        for l in range(m + 1, modes):
            a = math.sqrt((4.0 * l * l - 1) / (l * l - m * m))
            b = math.sqrt(max((l - 1.0) ** 2 - m * m, 0.0) / (4.0 * (l - 1.0) ** 2 - 1)) if l > 1 else 0.0
            earlier = table[m, l - 2] if l > m + 1 else 0.0
            table[m, l] = a * (cosine * table[m, l - 1] - b * earlier)
    quadrature = 2 * np.pi**2 * sine / lat_count
    return table, table * quadrature


def split_numpy(table):
    high = table.astype(np.float32).astype(jnp.bfloat16)
    low = (table - high.astype(np.float64)).astype(np.float32).astype(jnp.bfloat16)
    return high, low


@functools.lru_cache(maxsize=None)
def constant_tables(lat_count, lon_count, modes):
    pairs = modes // 2
    n = np.arange(lon_count)
    k = np.arange(modes)
    phase = 2 * np.pi * ((k[:, None] * n[None, :]) % lon_count) / lon_count
    trig = np.stack([np.cos(phase), -np.sin(phase)], axis=1)
    by_row = trig.reshape(2, pairs, 2, lon_count).transpose(0, 2, 1, 3).reshape(2 * modes, lon_count)
    forward = np.zeros((2 * modes, LANES))
    forward[:, :lon_count] = by_row / lon_count
    high, low = split_numpy(forward)
    forward = np.concatenate([high, high, low], axis=1)
    factor = np.where(k == 0, 1.0, 2.0)
    scaled = (trig * factor[:, None, None]).reshape(2, pairs, 2, lon_count).transpose(0, 2, 1, 3)
    scaled = scaled.reshape(2 * modes, lon_count)
    back = np.zeros((LANES, LANES))
    back[: 2 * modes, :lon_count] = scaled
    back[: 2 * modes, lon_count : lon_count + 2] = scaled[:, :2]
    back[: 2 * modes, LANES - 2 :] = scaled[:, lon_count - 2 :]
    high, low = split_numpy(back)
    back = np.concatenate([high, high, low], axis=0)
    table, weighted = legendre_numpy(modes, lat_count)
    into = np.zeros((pairs, LANES, LANES))
    onto = np.zeros((pairs, LANES, LANES))
    for s in range(2):
        part = slice(s * pairs, (s + 1) * pairs)
        lat, deg = slice(s * HALF, s * HALF + lat_count), slice(s * HALF, s * HALF + modes)
        into[:, lat, deg] = np.swapaxes(weighted[part], 1, 2)
        onto[:, deg, lat] = table[part]
    into = np.concatenate(split_numpy(into), axis=2)
    onto = np.concatenate(split_numpy(onto), axis=2)
    return forward, back, into, onto


def halves(value):
    high = value.astype(bf16)
    return high, (value - high.astype(f32)).astype(bf16)


def mm(a, b):
    return jnp.dot(a, b, preferred_element_type=f32)


def mm_wide(value, table):
    count = value.shape[0]
    high, low = halves(value)
    out = mm(jnp.concatenate([high, low], axis=0), table)
    return (out[:count, :LANES] + out[count:, :LANES]) + (out[:count, LANES:] + out[count:, LANES:])


def chunk_list(per):
    chunks = [(start, TILE) for start in range(0, per - per % TILE, TILE)]
    if per % TILE:
        chunks.append((per - per % TILE, per % TILE))
    return chunks


def block_kernel(
    nl, nj, rows, modes,
    latent, conv_first, conv_second, gains, norm_gain, fwd_hbm, back_hbm, into_hbm, onto_hbm, up_hbm, down_hbm,
    out,
    grid, sent, got, field, first, second, spec_in, spec_out, back_out, home, third,
    tap_one, tap_two, tap_col, taps, gain_in, gain_wide, gain_col, norm_in, fwd, back, into, onto, up, down,
    load_sem, in_sem, own_a, own_z, a_s, a_r, z_s, z_r,
):
    channels = latent.shape[1]
    cols = latent.shape[0] // rows
    blocks = channels // LANES
    total = nl * nj
    per = channels // total
    chunks = chunk_list(per)
    halves_count = rows // GROUP
    lat_count = rows * nl
    lon_count = cols * nj
    pairs = modes // 2
    la, lo = lax.axis_index("lat"), lax.axis_index("lon")
    me = lo * nl + la

    share = nl * per
    z_at, core = la // 2, lax.rem(la, 2)
    across = nl // 2

    def start_of(k, a):
        start, count = chunks[k]
        if per % TILE == 0:
            return a * per + start
        odd = lax.rem(a, 2)
        if count == TILE:
            return pl.multiple_of(a * per + odd * (per % TILE) + start, TILE)
        return a * per + (1 - odd) * start

    def rows_sent(k):
        return TILE - 1 if chunks[k][1] == TILE else chunks[k][1]

    def channels_of(k, a, b):
        return (slice(None), b, pl.ds(start_of(k, a), rows_sent(k)), slice(None))

    def place_of(k, a, b):
        count = chunks[k][1]
        bands = nl * count // TILE
        return (lax.rem(a, bands), b, slice(None), pl.ds(k * TILE + a // bands * count, rows_sent(k)), slice(None))

    def lanes(block):
        return pl.ds(block * LANES, LANES)

    def tile(start):
        return pl.ds(start if isinstance(start, int) else pl.multiple_of(start, TILE), TILE)

    def rcopy(src, dst, send, recv, a, b):
        return pltpu.make_async_remote_copy(
            src_ref=src, dst_ref=dst, send_sem=send, recv_sem=recv,
            device_id={"lat": a, "lon": b}, device_id_type=pl.DeviceIdType.MESH,
        )

    def others(action):
        for d in range(1, nj):
            action(la, lax.rem(lo + d, nj))

        def step(d, carry):
            a = lax.rem(la + d, nl)
            for b in range(nj):
                action(a, lax.rem(lo + b, nj))
            return carry

        lax.fori_loop(1, nl, step, 0)

    lane = lax.broadcasted_iota(jnp.int32, (TILE, LANES), 1)
    sublane = lax.broadcasted_iota(jnp.int32, (TILE, LANES), 0)
    within = lax.rem(lane, SLOT)
    wide = SLOT - cols
    room = len(chunks) * TILE
    by_owner = lambda ref: ref.reshape(halves_count, nj, share, LANES)
    by_band = lambda ref: ref.reshape(nl, nj, halves_count, room, LANES)

    def turned(row, shift):
        return pltpu.roll(row, shift % LANES, 1) if shift % LANES else row

    def fold(ref, start, stride):
        places = [pl.ds(start + c, TILE, stride=stride) for c in range(TILE)]
        lines = [ref[at, :] for at in places]
        for c in range(TILE - 1):
            ref[places[c], :] = jnp.where(within >= cols, turned(lines[-1], cols - wide * c), lines[c])

    def unfold(ref, start, stride):
        last = None
        for c in reversed(range(TILE - 1)):
            moved = turned(ref[pl.ds(start + c, TILE, stride=stride), :], wide * c - cols)
            last = moved if last is None else jnp.where(within < wide * (c + 1), moved, last)
        ref[pl.ds(start + TILE - 1, TILE, stride=stride), :] = last

    def owner_tiles(k, h, action, ref):
        odd = per % TILE
        step = 2 * per if odd else per
        for parity in range(step // per):
            base = h * channels + parity * (per + odd) + chunks[k][0]
            for group in range(channels // step // TILE):
                action(ref, base + group * TILE * step, step)

    def band_tiles(k, a, action, ref):
        action(ref, a * nj * halves_count * room + k * TILE, room)

    def whole_tile(k):
        return chunks[k][1] == TILE

    barrier = pltpu.get_barrier_semaphore()
    others(
        lambda a, b: pl.semaphore_signal(
            barrier, inc=1, device_id={"lat": a, "lon": b}, device_id_type=pl.DeviceIdType.MESH
        )
    )

    pairs_of = (
        (conv_first, tap_one), (conv_second, tap_two), (gains, gain_in),
        (norm_gain, norm_in), (fwd_hbm, fwd), (back_hbm, back), (into_hbm, into), (onto_hbm, onto),
        (up_hbm, up), (down_hbm, down),
    )
    loads = [pltpu.make_async_copy(a, b, load_sem.at[i]) for i, (a, b) in enumerate(pairs_of)]

    def in_copy(block):
        return pltpu.make_async_copy(
            latent.at[:, lanes(block)], grid.at[block, pl.ds(0, rows * cols)], in_sem.at[block]
        )

    for block in range(blocks):
        in_copy(block).start()

    for block in range(blocks):
        grid[block, rows * cols :, :] = jnp.zeros((rows * (SLOT - cols), LANES), f32)

    for block in range(blocks):
        in_copy(block).wait()
        if block + 1 == blocks:
            for load in loads:
                load.start()
        for h in range(halves_count):
            parts = [grid[block, pl.ds(h * GROUP + i, SLOT, stride=rows), :] for i in range(GROUP)]
            block_rows = jnp.concatenate(parts, axis=0).T
            sent[h * channels + block * LANES : h * channels + (block + 1) * LANES, :] = block_rows
    for k in range(len(chunks)):
        if whole_tile(k):
            for h in range(halves_count):
                owner_tiles(k, h, fold, sent)

    def a_copy(k, a, b):
        return rcopy(by_owner(sent).at[channels_of(k, a, b)], by_band(got).at[place_of(k, la, lo)], a_s.at[k], a_r.at[k], a, b)

    def z_copy(k, a, b):
        return rcopy(by_band(back_out).at[place_of(k, a, b)], by_owner(home).at[channels_of(k, la, lo)], z_s.at[k], z_r.at[k], a, b)

    def own_in(k):
        return pltpu.make_async_copy(by_owner(sent).at[channels_of(k, la, lo)], by_band(got).at[place_of(k, la, lo)], own_a.at[k])

    def own_back(k):
        return pltpu.make_async_copy(by_band(back_out).at[place_of(k, la, lo)], by_owner(home).at[channels_of(k, la, lo)], own_z.at[k])

    def everyone(k, send, recv):
        whole = first.at[0, pl.ds(0, (total - 1) * halves_count * rows_sent(k))]
        return rcopy(whole, whole, send.at[k], recv.at[k], lax.rem(la + 1, nl), lo)

    def spread(k, copy):
        def band(d, flip, start):
            a = lax.rem(z_at + d, across) * 2 + (1 - core if flip else core)
            for b in range(start, nj):
                copy(k, a, lax.rem(lo + b, nj)).start()

        for d in [0] + [e for q in range(1, across // 2 + 1) for e in sorted({q, across - q})]:
            band(d, False, 1 if d == 0 else 0)
            band(d, True, 0)

    pl.semaphore_wait(barrier, total - 1)
    def send_in(k):
        spread(k, a_copy)
        own_in(k).start()

    for k in range(len(chunks)):
        send_in(k)

    loads[0].wait()
    loads[1].wait()
    loads[2].wait()
    gain_wide[...] = jnp.zeros_like(gain_wide)
    gain_wide[0:modes, :] = gain_in[...]
    gain_wide[HALF : HALF + modes, :] = gain_in[...]
    width = gain_in.shape[1]
    for start in range(0, width, LANES):
        stop = min(start + LANES, width)
        gain_col[start:stop, :] = gain_wide[:, start:stop].T
    for s, source in enumerate((tap_one, tap_two)):
        for block in range(blocks):
            square = jnp.concatenate([source[:, lanes(block)], jnp.zeros((7, LANES), f32)], axis=0)
            tap_col[s, lanes(block), :] = square.T
        for k, (_, count) in enumerate(chunks):
            own = tap_col[s, pl.ds(lo * share + start_of(k, la), TILE), :]
            if count < TILE:
                own = jnp.concatenate([own[:count]] * (TILE // count), axis=0)
            for t in range(25):
                taps[s, k, t] = jnp.broadcast_to(own[:, t : t + 1], (TILE, LANES))

    low_half = lax.broadcasted_iota(jnp.int32, (pairs, LANES), 1) < HALF

    def unpack(k):
        if whole_tile(k):
            for a in range(nl):
                band_tiles(k, a, unfold, got)
        for a in range(nl * chunks[k][1] // TILE):
            for h in range(halves_count):
                pieces = [got[tile(((a * nj + b) * halves_count + h) * room + k * TILE), :] for b in range(nj)]
                for i in range(GROUP):
                    row = turned(pieces[nj - 1], LANES - cols - SLOT * i)
                    row = jnp.where(lane < LANES - 4, turned(pieces[0], lon_count - SLOT * i), row)
                    for b in reversed(range(nj)):
                        row = jnp.where(lane < cols * (b + 1), turned(pieces[b], cols * b - SLOT * i), row)
                    field[k, tile((a * rows + h * GROUP + i + 2) * TILE), :] = row
        edges(field, k)

    def edges(padded, k):
        count = chunks[k][1]
        lines = lat_count * count // TILE
        for j in range(2):
            above, below = padded[k, tile((lines + j) * TILE), :], padded[k, tile((2 + j) * TILE), :]
            blank = jnp.zeros_like(above)
            if count < TILE:
                above = jnp.where(sublane >= count, pltpu.roll(above, count, 0), blank)
                below = jnp.where(sublane < TILE - count, pltpu.roll(below, TILE - count, 0), blank)
            else:
                above = below = blank
            padded[k, tile(j * TILE), :] = above
            padded[k, tile((lines + 2 + j) * TILE), :] = below

    def stencil(source, s, k, emit):
        step_rows = TILE
        for g in range(lat_count * chunks[k][1] // TILE // step_rows):
            base = g * step_rows
            lines = [source[k, tile((base + j) * TILE), :] for j in range(step_rows + 4)]
            sums = [lines[j + 2] for j in range(step_rows)]
            for b in range(5):
                weights = [taps[s, k, a * 5 + b] for a in range(5)]
                for j in range(step_rows):
                    term = weights[0] * lines[j]
                    for a in range(1, 5):
                        term = term + weights[a] * lines[j + a]
                    sums[j] = sums[j] + turned(term, 2 - b)
            emit(g, base, sums)

    def lines_of(k, c, skip):
        count = chunks[k][1]
        lines = lat_count * count // TILE
        return [pl.ds(skip * TILE + q * count + c, lines, stride=TILE) for q in range(TILE // count)]

    def transform(k):
        count = chunks[k][1]
        by_channel = jnp.concatenate(
            [first[k, at, :] for c in range(count) for at in lines_of(k, c, 0)], axis=0
        )
        high, low = halves(by_channel)
        coeffs = lax.dot_general(
            fwd[...], jnp.concatenate([high, low, high], axis=1), (((1,), (1,)), ((), ())),
            preferred_element_type=f32,
        )
        for p in range(count // 2):
            for r in range(2):
                part = [coeffs[(2 * s + r) * pairs : (2 * s + r + 1) * pairs, lanes_of(p)] for s in range(2)]
                even = jnp.where(low_half, part[0], pltpu.roll(part[1], HALF, 1))
                odd = jnp.where(low_half, pltpu.roll(part[0], HALF, 1), part[1])
                spec_in[k, pl.ds(r * TILE + 2 * p, pairs, stride=2 * TILE), :] = even
                spec_in[k, pl.ds(r * TILE + 2 * p + 1, pairs, stride=2 * TILE), :] = odd

    def lanes_of(p):
        return slice(p * LANES, (p + 1) * LANES)

    def degrees(k):
        gain = gain_col[pl.ds(start_of(k, la), TILE), :]
        gain = jnp.concatenate([gain, gain], axis=0)
        for m in range(pairs):
            at = pl.ds(m * 2 * TILE, 2 * TILE)
            spectrum = mm_wide(spec_in[k, at, :], into[m]) * gain
            spec_out[k, at, :] = mm_wide(spectrum, onto[m])

    def synthesis(k):
        count = chunks[k][1]
        rows_of = [[None] * (count // 2) for _ in range(4)]
        for p in range(count // 2):
            for r in range(2):
                even = spec_out[k, pl.ds(r * TILE + 2 * p, pairs, stride=2 * TILE), :]
                odd = spec_out[k, pl.ds(r * TILE + 2 * p + 1, pairs, stride=2 * TILE), :]
                rows_of[r][p] = jnp.where(low_half, even, pltpu.roll(odd, HALF, 1))
                rows_of[2 + r][p] = jnp.where(low_half, pltpu.roll(even, HALF, 1), odd)
        blank = jnp.zeros((LANES - 4 * pairs, LANES), f32)
        for p in range(count // 2):
            square = jnp.concatenate([rows_of[q][p] for q in range(4)] + [blank], axis=0).T
            high, low = halves(square)
            values = mm(jnp.concatenate([high, low, high], axis=1), back[...])
            for e in range(2):
                places = list(zip(lines_of(k, 2 * p + e, 0), lines_of(k, 2 * p + e, 2)))
                lines = lat_count // len(places)
                for q, (before, after) in enumerate(places):
                    base = e * lat_count + q * lines
                    second[k, after, :] = first[k, before, :] + values[base : base + lines]
        edges(second, k)

    def emit_first(k):
        def emit(g, base, sums):
            for j, row in enumerate(sums):
                first[k, tile((base + j) * TILE), :] = row
        return emit

    def emit_second(k):
        def emit(a, base, sums):
            for h in range(halves_count):
                for b in range(nj):
                    packed = None
                    for i in reversed(range(GROUP)):
                        moved = turned(sums[h * GROUP + i], SLOT * i - cols * b)
                        packed = moved if packed is None else jnp.where(lane < SLOT * (i + 1), moved, packed)
                    back_out[tile(((a * nj + b) * halves_count + h) * room + k * TILE), :] = packed
        return emit

    for k in range(len(chunks)):
        everyone(k, a_s, a_r).wait_recv()
        own_in(k).wait()
        unpack(k)
        stencil(field, 0, k, emit_first(k))
        if k == 0:
            loads[4].wait()
        transform(k)
        if k == 0:
            loads[6].wait()
            loads[7].wait()
        degrees(k)
        if k == 0:
            loads[5].wait()
        synthesis(k)
        stencil(second, 1, k, emit_second(k))
        if whole_tile(k):
            for a in range(nl):
                band_tiles(k, a, fold, back_out)
        spread(k, z_copy)
        own_back(k).start()

    loads[3].wait()
    loads[8].wait()
    loads[9].wait()
    for k in range(len(chunks)):
        everyone(k, z_s, z_r).wait_recv()
        own_back(k).wait()
        if whole_tile(k):
            for h in range(halves_count):
                owner_tiles(k, h, unfold, home)
    for h in range(halves_count):
        for block in range(blocks):
            third[pl.ds(h * LANES, LANES), lanes(block)] = (
                home[h * channels + block * LANES : h * channels + (block + 1) * LANES, :].T
            )
    state = third[...]
    average = jnp.mean(state, axis=-1, keepdims=True)
    centred = state - average
    spread = jnp.mean(centred * centred, axis=-1, keepdims=True)
    normed = (centred * lax.rsqrt(spread + 1e-05) * norm_in[...].reshape(1, channels)).astype(bf16)
    active = jax.nn.gelu(mm(normed, up[...]), approximate=True).astype(bf16)
    result = state + mm(active, down[...])
    for block in range(blocks):
        for i in range(rows):
            grid[block, pl.ds(i, cols, stride=rows), :] = (
                result[SLOT * i : SLOT * i + cols, block * LANES : (block + 1) * LANES]
            )
        out[:, lanes(block)] = grid[block, 0 : rows * cols, :]
    for k in range(len(chunks)):
        everyone(k, a_s, a_r).wait_send()
        everyone(k, z_s, z_r).wait_send()


def fused(nl, nj, latent, conv_first, conv_second, filter_gains, norm_gain, up_weight, down_weight):
    rows, cols, channels = latent.shape
    modes, width = filter_gains.shape
    lat_count, lon_count = rows * nl, cols * nj
    forward, back, into, onto = (jnp.asarray(t) for t in constant_tables(lat_count, lon_count, modes))
    blocks = channels // LANES
    per = channels // (nl * nj)
    count = len(chunk_list(per))
    room = count * TILE
    halves_count = rows // GROUP
    vm = lambda *shape, kind=f32: pltpu.VMEM(shape, kind)
    dma = lambda *shape: pltpu.SemaphoreType.DMA(shape)
    far = pl.BlockSpec(memory_space=pltpu.HBM)
    result = pl.pallas_call(
        functools.partial(block_kernel, nl, nj, rows, modes),
        out_shape=pltpu.VMEM((cols * rows, channels), f32),
        in_specs=[far] * 11,
        out_specs=pl.BlockSpec(memory_space=pltpu.VMEM),
        scratch_shapes=[
            vm(blocks, rows * SLOT, LANES),
            vm(halves_count * channels, LANES),
            vm(nl * nj * halves_count * room, LANES),
            vm(count, (lat_count + 4) * TILE, LANES),
            vm(count, lat_count * TILE, LANES),
            vm(count, (lat_count + 4) * TILE, LANES),
            vm(count, modes * TILE, LANES),
            vm(count, modes * TILE, LANES),
            vm(nl * nj * halves_count * room, LANES),
            vm(halves_count * channels, LANES),
            vm(rows * SLOT, channels),
            vm(25, channels),
            vm(25, channels),
            vm(2, channels + TILE, 32),
            vm(2, count, 25, TILE, LANES),
            vm(modes, width),
            vm(LANES, width),
            vm(width + TILE, LANES),
            vm(channels),
            vm(*forward.shape, kind=bf16),
            vm(*back.shape, kind=bf16),
            vm(*into.shape, kind=bf16),
            vm(*onto.shape, kind=bf16),
            vm(*up_weight.shape, kind=bf16),
            vm(*down_weight.shape, kind=bf16),
            dma(10), dma(blocks), dma(count), dma(count),
            dma(count), dma(count), dma(count), dma(count),
        ],
        compiler_params=pltpu.CompilerParams(
            collective_id=0, has_side_effects=True, vmem_limit_bytes=60 * 1024 * 1024
        ),
        name="block",
    )(
        jnp.swapaxes(latent, 0, 1).reshape(cols * rows, channels), conv_first, conv_second,
        filter_gains, norm_gain, forward, back, into, onto, up_weight, down_weight,
    )
    return jnp.swapaxes(result.reshape(cols, rows, channels), 0, 1)


def fits(nl, nj, latent, filter_gains):
    rows, cols, channels = latent.shape
    modes = filter_gains.shape[0]
    total = nl * nj
    if rows != TILE or channels % LANES or channels % total or nj < 2 or nl < 2:
        return False
    if (channels // total) % GROUP or nl % 4 or rows * nl != HALF or cols > SLOT or cols != (TILE - 1) * (SLOT - cols) or (channels // (2 * channels // total)) % TILE or cols * nj > LANES - 8 or cols < 4:
        return False
    return modes % 16 == 0 and modes <= HALF and 2 * modes <= LANES


def body(latent, conv_first, conv_second, filter_gains, norm_gain, up_weight, down_weight):
    nl, nj = lax.axis_size("lat"), lax.axis_size("lon")
    arguments = (latent, conv_first, conv_second, filter_gains, norm_gain, up_weight, down_weight)
    if fits(nl, nj, latent, filter_gains):
        return fused(nl, nj, *arguments)
    return per_device(*arguments)


def solution(mesh):
    return jax.shard_map(
        body,
        mesh=mesh,
        in_specs=(P("lat", "lon", None), P(), P(), P(None, "lon"), P(), P(), P()),
        out_specs=P("lat", "lon", None),
        check_vma=False,
    )
```

```python
import functools
import math

import jax
import jax.numpy as jnp
import numpy as np
from jax import lax
from jax.experimental import pallas as pl
from jax.experimental.pallas import tpu as pltpu
from jax.sharding import PartitionSpec as P

highest = lax.Precision.HIGHEST


def padded_2(block, sides, width):
    for axis, dim in sides:
        count = lax.axis_size(axis)
        forward = [(i, i + 1) for i in range(count - 1)]
        backward = [(target, source) for source, target in forward]
        low = lax.ppermute(
            lax.slice_in_dim(block, block.shape[dim] - width, None, axis=dim), axis, forward
        )
        high = lax.ppermute(lax.slice_in_dim(block, 0, width, axis=dim), axis, backward)
        block = jnp.concatenate([low, block, high], axis=dim)
    return block


def stencil_sum(padded, weights, row_count, col_count):
    stencil_total = jnp.zeros((row_count, col_count, padded.shape[2]), padded.dtype)
    for row_shift in range(5):
        for col_shift in range(5):
            stencil_total = (
                stencil_total
                + weights[row_shift * 5 + col_shift]
                * padded[row_shift : row_shift + row_count, col_shift : col_shift + col_count, :]
            )
    return stencil_total


def slice_stencil(sliced, weights):
    lat_extended = padded_2(sliced, (("lat", 0),), 2)
    wrapped = jnp.concatenate([lat_extended[:, -2:], lat_extended, lat_extended[:, :2]], axis=1)
    return stencil_sum(wrapped, weights, sliced.shape[0], sliced.shape[1])


def colatitude(cell_count, float_type):
    cell_index = jnp.arange(cell_count).astype(float_type)
    return jnp.pi * (cell_index + 0.5) / cell_count


def legendre_table(orders, degrees, cosine, sine_theta):
    log_seed = 0.5 * (
        jnp.log((2.0 * orders + 1.0) / (4.0 * jnp.pi))
        + jax.scipy.special.gammaln(2.0 * orders + 1.0)
        - 2.0 * orders * jnp.log(2.0)
        - 2.0 * jax.scipy.special.gammaln(orders + 1.0)
    )
    diagonal_term = jnp.exp(log_seed[:, None] + orders[:, None] * jnp.log(sine_theta)[None, :])
    blanks = jnp.zeros_like(diagonal_term)
    legendre = jnp.zeros((orders.shape[0], degrees, sine_theta.shape[0]), diagonal_term.dtype)

    def block_step(block_index, state_tuple):
        previous, earlier, legendre = state_tuple
        values = []
        for offset in range(8):
            degree = (block_index * 8 + offset).astype(diagonal_term.dtype)
            square = degree * degree
            upper_ratio = jnp.sqrt(
                jnp.maximum(4.0 * square - 1.0, 1.0) / jnp.maximum(square - orders * orders, 1.0)
            )
            below_sq = (degree - 1.0) * (degree - 1.0)
            lower_ratio = jnp.sqrt(
                jnp.maximum(below_sq - orders * orders, 0.0)
                / jnp.maximum(4.0 * below_sq - 1.0, 1.0)
            )
            recurred = upper_ratio[:, None] * (
                cosine[None, :] * previous - lower_ratio[:, None] * earlier
            )
            current = jnp.where(
                (degree < orders)[:, None],
                blanks,
                jnp.where((degree == orders)[:, None], diagonal_term, recurred),
            )
            values.append(current)
            earlier = previous
            previous = current
        stacked = jnp.stack(values, axis=1)
        legendre = lax.dynamic_update_slice(
            legendre, stacked, (jnp.int32(0), (block_index * 8).astype(jnp.int32), jnp.int32(0))
        )
        return (previous, earlier, legendre)

    return lax.fori_loop(0, degrees // 8, block_step, (blanks, blanks, legendre))[2]


def fourier_tables(lon_count, mode_count, float_type):
    product_index = jnp.arange(lon_count)[:, None] * jnp.arange(mode_count)[None, :] % lon_count
    phase_grid = 2.0 * jnp.pi * product_index.astype(float_type) / lon_count
    forward = jnp.stack([jnp.cos(phase_grid), -jnp.sin(phase_grid)], axis=1) / lon_count
    factor = jnp.where(jnp.arange(mode_count) == 0, 1.0, 2.0).astype(float_type)
    inverse = jnp.stack(
        [jnp.cos(phase_grid).T * factor[:, None], -jnp.sin(phase_grid).T * factor[:, None]], axis=0
    )
    return (forward, inverse)


def channel_mlp(latent, norm_gain, up_weight, down_weight):
    average = jnp.mean(latent, axis=-1, keepdims=True)
    centred = latent - average
    spread = jnp.mean(centred * centred, axis=-1, keepdims=True)
    normed = (centred * lax.rsqrt(spread + 1e-05) * norm_gain).astype(jnp.bfloat16)
    hidden = jnp.dot(normed, up_weight, preferred_element_type=jnp.float32)
    active = jax.nn.gelu(hidden, approximate=True).astype(jnp.bfloat16)
    return latent + jnp.dot(active, down_weight, preferred_element_type=jnp.float32)


def per_device(latent, conv_first, conv_second, filter_gains, norm_gain, up_weight, down_weight):
    lat_size = lax.axis_size("lat")
    lon_size = lax.axis_size("lon")
    lat_local = latent.shape[0]
    lon_local = latent.shape[1]
    slice_width = filter_gains.shape[1]
    mode_count = filter_gains.shape[0]
    lat_count = lat_local * lat_size
    lon_count = lon_local * lon_size
    order_count = mode_count // lat_size
    channel_start = lax.axis_index("lon") * slice_width
    sliced = lax.all_to_all(latent, "lon", split_axis=2, concat_axis=1, tiled=True)
    first_taps = lax.dynamic_slice_in_dim(conv_first, channel_start, slice_width, 1)
    first_sliced = sliced + slice_stencil(sliced, first_taps)
    forward, inverse = fourier_tables(lon_count, mode_count, jnp.float32)
    colat_grid = colatitude(lat_count, jnp.float32)
    orders = (lax.axis_index("lat") * order_count + jnp.arange(order_count)).astype(jnp.float32)
    legendre = legendre_table(orders, mode_count, jnp.cos(colat_grid), jnp.sin(colat_grid))
    quadrature = 2.0 * jnp.pi * jnp.pi * jnp.sin(colat_grid) / lat_count
    weighted = legendre * quadrature
    coeffs = jnp.einsum("inc,nrk->irkc", first_sliced, forward, precision=highest)
    spectrum = jnp.einsum(
        "kli,irkc->lrkc",
        weighted,
        lax.all_to_all(coeffs, "lat", split_axis=2, concat_axis=0, tiled=True),
        precision=highest,
    )
    spectrum = spectrum * filter_gains[:, None, None, :]
    restored = jnp.einsum("kli,lrkc->irkc", legendre, spectrum, precision=highest)
    returned = lax.all_to_all(restored, "lat", split_axis=0, concat_axis=2, tiled=True)
    filtered = jnp.einsum("irkc,rkn->inc", returned, inverse, precision=highest)
    second_taps = lax.dynamic_slice_in_dim(conv_second, channel_start, slice_width, 1)
    second_sliced = first_sliced + filtered
    incoming = second_sliced + slice_stencil(second_sliced, second_taps)
    arrived = lax.all_to_all(incoming, "lon", split_axis=1, concat_axis=2, tiled=True)
    return channel_mlp(arrived, norm_gain, up_weight, down_weight)


LANES = 128
TILE = 8
GROUP = 4
SLOT = LANES // GROUP
HALF = LANES // 2
bf16 = jnp.bfloat16
f32 = jnp.float32


def legendre_numpy(modes, lat_count):
    theta = np.pi * (np.arange(lat_count) + 0.5) / lat_count
    cosine, sine = np.cos(theta), np.sin(theta)
    table = np.zeros((modes, modes, lat_count))
    for m in range(modes):
        seed = 0.5 * (
            math.log((2 * m + 1) / (4 * math.pi))
            + math.lgamma(2 * m + 1)
            - 2 * m * math.log(2.0)
            - 2 * math.lgamma(m + 1)
        )
        table[m, m] = np.exp(seed + m * np.log(sine))
        for l in range(m + 1, modes):
            a = math.sqrt((4.0 * l * l - 1) / (l * l - m * m))
            b = math.sqrt(max((l - 1.0) ** 2 - m * m, 0.0) / (4.0 * (l - 1.0) ** 2 - 1)) if l > 1 else 0.0
            earlier = table[m, l - 2] if l > m + 1 else 0.0
            table[m, l] = a * (cosine * table[m, l - 1] - b * earlier)
    quadrature = 2 * np.pi**2 * sine / lat_count
    return table, table * quadrature


def split_numpy(table):
    high = table.astype(np.float32).astype(jnp.bfloat16)
    low = (table - high.astype(np.float64)).astype(np.float32).astype(jnp.bfloat16)
    return high, low


@functools.lru_cache(maxsize=None)
def constant_tables(lat_count, lon_count, modes):
    pairs = modes // 2
    n = np.arange(lon_count)
    k = np.arange(modes)
    phase = 2 * np.pi * ((k[:, None] * n[None, :]) % lon_count) / lon_count
    trig = np.stack([np.cos(phase), -np.sin(phase)], axis=1)
    by_row = trig.reshape(2, pairs, 2, lon_count).transpose(0, 2, 1, 3).reshape(2 * modes, lon_count)
    forward = np.zeros((2 * modes, LANES))
    forward[:, :lon_count] = by_row / lon_count
    high, low = split_numpy(forward)
    forward = np.concatenate([high, high, low], axis=1)
    factor = np.where(k == 0, 1.0, 2.0)
    scaled = (trig * factor[:, None, None]).reshape(2, pairs, 2, lon_count).transpose(0, 2, 1, 3)
    scaled = scaled.reshape(2 * modes, lon_count)
    back = np.zeros((LANES, LANES))
    back[: 2 * modes, :lon_count] = scaled
    back[: 2 * modes, lon_count : lon_count + 2] = scaled[:, :2]
    back[: 2 * modes, LANES - 2 :] = scaled[:, lon_count - 2 :]
    high, low = split_numpy(back)
    back = np.concatenate([high, high, low], axis=0)
    table, weighted = legendre_numpy(modes, lat_count)
    into = np.zeros((pairs, LANES, LANES))
    onto = np.zeros((pairs, LANES, LANES))
    for s in range(2):
        part = slice(s * pairs, (s + 1) * pairs)
        lat, deg = slice(s * HALF, s * HALF + lat_count), slice(s * HALF, s * HALF + modes)
        into[:, lat, deg] = np.swapaxes(weighted[part], 1, 2)
        onto[:, deg, lat] = table[part]
    into = np.concatenate(split_numpy(into), axis=2)
    onto = np.concatenate(split_numpy(onto), axis=2)
    return forward, back, into, onto


def halves(value):
    high = value.astype(bf16)
    return high, (value - high.astype(f32)).astype(bf16)


def mm(a, b):
    return jnp.dot(a, b, preferred_element_type=f32)


def mm_wide(value, table):
    count = value.shape[0]
    high, low = halves(value)
    out = mm(jnp.concatenate([high, low], axis=0), table)
    return (out[:count, :LANES] + out[count:, :LANES]) + (out[:count, LANES:] + out[count:, LANES:])


def chunk_list(per):
    chunks = [(start, TILE) for start in range(0, per - per % TILE, TILE)]
    if per % TILE:
        chunks.append((per - per % TILE, per % TILE))
    return chunks[-1:] + chunks[:-1]


def block_kernel(
    nl, nj, rows, modes,
    latent, conv_first, conv_second, gains, norm_gain, fwd_hbm, back_hbm, into_hbm, onto_hbm, up_hbm, down_hbm,
    out,
    grid, sent, got, field, first, second, spec_in, spec_out, back_out, home, third,
    tap_one, tap_two, tap_col, taps, gain_in, gain_wide, gain_col, norm_in, fwd, back, into, onto, up, down,
    load_sem, in_sem, own_a, own_z, a_s, a_r, z_s, z_r,
):
    channels = latent.shape[1]
    cols = latent.shape[0] // rows
    blocks = channels // LANES
    total = nl * nj
    per = channels // total
    chunks = chunk_list(per)
    halves_count = rows // GROUP
    lat_count = rows * nl
    lon_count = cols * nj
    pairs = modes // 2
    la, lo = lax.axis_index("lat"), lax.axis_index("lon")
    me = lo * nl + la

    share = nl * per
    z_at, core = la // 2, lax.rem(la, 2)
    across = nl // 2

    def start_of(k, a):
        start, count = chunks[k]
        if per % TILE == 0:
            return a * per + start
        odd = lax.rem(a, 2)
        if count == TILE:
            return pl.multiple_of(a * per + odd * (per % TILE) + start, TILE)
        return a * per + (1 - odd) * start

    def rows_sent(k):
        return TILE - 1 if chunks[k][1] == TILE else chunks[k][1]

    def channels_of(k, a, b):
        return (slice(None), b, pl.ds(start_of(k, a), rows_sent(k)), slice(None))

    def place_of(k, a, b):
        count = chunks[k][1]
        bands = nl * count // TILE
        return (lax.rem(a, bands), b, slice(None), pl.ds(k * TILE + a // bands * count, rows_sent(k)), slice(None))

    def lanes(block):
        return pl.ds(block * LANES, LANES)

    def tile(start):
        return pl.ds(start if isinstance(start, int) else pl.multiple_of(start, TILE), TILE)

    def rcopy(src, dst, send, recv, a, b):
        return pltpu.make_async_remote_copy(
            src_ref=src, dst_ref=dst, send_sem=send, recv_sem=recv,
            device_id={"lat": a, "lon": b}, device_id_type=pl.DeviceIdType.MESH,
        )

    def others(action):
        for d in range(1, nj):
            action(la, lax.rem(lo + d, nj))

        def step(d, carry):
            a = lax.rem(la + d, nl)
            for b in range(nj):
                action(a, lax.rem(lo + b, nj))
            return carry

        lax.fori_loop(1, nl, step, 0)

    lane = lax.broadcasted_iota(jnp.int32, (TILE, LANES), 1)
    sublane = lax.broadcasted_iota(jnp.int32, (TILE, LANES), 0)
    within = lax.rem(lane, SLOT)
    wide = SLOT - cols
    room = len(chunks) * TILE
    by_owner = lambda ref: ref.reshape(halves_count, nj, share, LANES)
    by_band = lambda ref: ref.reshape(nl, nj, halves_count, room, LANES)

    def turned(row, shift):
        return pltpu.roll(row, shift % LANES, 1) if shift % LANES else row

    def fold(ref, start, stride):
        places = [pl.ds(start + c, TILE, stride=stride) for c in range(TILE)]
        lines = [ref[at, :] for at in places]
        for c in range(TILE - 1):
            ref[places[c], :] = jnp.where(within >= cols, turned(lines[-1], cols - wide * c), lines[c])

    def unfold(ref, start, stride):
        last = None
        for c in reversed(range(TILE - 1)):
            moved = turned(ref[pl.ds(start + c, TILE, stride=stride), :], wide * c - cols)
            last = moved if last is None else jnp.where(within < wide * (c + 1), moved, last)
        ref[pl.ds(start + TILE - 1, TILE, stride=stride), :] = last

    def owner_tiles(k, h, action, ref):
        odd = per % TILE
        step = 2 * per if odd else per
        for parity in range(step // per):
            base = h * channels + parity * (per + odd) + chunks[k][0]
            for group in range(channels // step // TILE):
                action(ref, base + group * TILE * step, step)

    def band_tiles(k, a, action, ref):
        action(ref, a * nj * halves_count * room + k * TILE, room)

    def whole_tile(k):
        return chunks[k][1] == TILE

    barrier = pltpu.get_barrier_semaphore()
    others(
        lambda a, b: pl.semaphore_signal(
            barrier, inc=1, device_id={"lat": a, "lon": b}, device_id_type=pl.DeviceIdType.MESH
        )
    )

    pairs_of = (
        (conv_first, tap_one), (conv_second, tap_two), (gains, gain_in),
        (norm_gain, norm_in), (fwd_hbm, fwd), (back_hbm, back), (into_hbm, into), (onto_hbm, onto),
        (up_hbm, up), (down_hbm, down),
    )
    loads = [pltpu.make_async_copy(a, b, load_sem.at[i]) for i, (a, b) in enumerate(pairs_of)]

    def in_copy(block):
        return pltpu.make_async_copy(
            latent.at[:, lanes(block)], grid.at[block, pl.ds(0, rows * cols)], in_sem.at[block]
        )

    for block in range(blocks):
        in_copy(block).start()

    for block in range(blocks):
        grid[block, rows * cols :, :] = jnp.zeros((rows * (SLOT - cols), LANES), f32)

    for block in range(blocks):
        in_copy(block).wait()
        if block + 1 == blocks:
            for load in loads:
                load.start()
        for h in range(halves_count):
            parts = [grid[block, pl.ds(h * GROUP + i, SLOT, stride=rows), :] for i in range(GROUP)]
            block_rows = jnp.concatenate(parts, axis=0).T
            sent[h * channels + block * LANES : h * channels + (block + 1) * LANES, :] = block_rows
    for k in range(len(chunks)):
        if whole_tile(k):
            for h in range(halves_count):
                owner_tiles(k, h, fold, sent)

    def a_copy(k, a, b):
        return rcopy(by_owner(sent).at[channels_of(k, a, b)], by_band(got).at[place_of(k, la, lo)], a_s.at[k], a_r.at[k], a, b)

    def z_copy(k, a, b):
        return rcopy(by_band(back_out).at[place_of(k, a, b)], by_owner(home).at[channels_of(k, la, lo)], z_s.at[k], z_r.at[k], a, b)

    def own_in(k):
        return pltpu.make_async_copy(by_owner(sent).at[channels_of(k, la, lo)], by_band(got).at[place_of(k, la, lo)], own_a.at[k])

    def own_back(k):
        return pltpu.make_async_copy(by_band(back_out).at[place_of(k, la, lo)], by_owner(home).at[channels_of(k, la, lo)], own_z.at[k])

    def everyone(k, send, recv):
        whole = first.at[0, pl.ds(0, (total - 1) * halves_count * rows_sent(k))]
        return rcopy(whole, whole, send.at[k], recv.at[k], lax.rem(la + 1, nl), lo)

    def spread(k, copy):
        def band(d, flip, start):
            a = lax.rem(z_at + d, across) * 2 + (1 - core if flip else core)
            for b in range(start, nj):
                copy(k, a, lax.rem(lo + b, nj)).start()

        for d in [0] + [e for q in range(1, across // 2 + 1) for e in sorted({q, across - q})]:
            band(d, False, 1 if d == 0 else 0)
            band(d, True, 0)

    pl.semaphore_wait(barrier, total - 1)
    def send_in(k):
        spread(k, a_copy)
        own_in(k).start()

    ahead = 2
    for k in range(ahead):
        send_in(k)

    loads[0].wait()
    loads[1].wait()
    loads[2].wait()
    gain_wide[...] = jnp.zeros_like(gain_wide)
    gain_wide[0:modes, :] = gain_in[...]
    gain_wide[HALF : HALF + modes, :] = gain_in[...]
    width = gain_in.shape[1]
    for start in range(0, width, LANES):
        stop = min(start + LANES, width)
        gain_col[start:stop, :] = gain_wide[:, start:stop].T
    for s, source in enumerate((tap_one, tap_two)):
        for block in range(blocks):
            square = jnp.concatenate([source[:, lanes(block)], jnp.zeros((7, LANES), f32)], axis=0)
            tap_col[s, lanes(block), :] = square.T
        for k, (_, count) in enumerate(chunks):
            own = tap_col[s, pl.ds(lo * share + start_of(k, la), TILE), :]
            if count < TILE:
                own = jnp.concatenate([own[:count]] * (TILE // count), axis=0)
            for t in range(25):
                taps[s, k, t] = jnp.broadcast_to(own[:, t : t + 1], (TILE, LANES))

    low_half = lax.broadcasted_iota(jnp.int32, (pairs, LANES), 1) < HALF

    def unpack(k):
        if whole_tile(k):
            for a in range(nl):
                band_tiles(k, a, unfold, got)
        for a in range(nl * chunks[k][1] // TILE):
            for h in range(halves_count):
                pieces = [got[tile(((a * nj + b) * halves_count + h) * room + k * TILE), :] for b in range(nj)]
                for i in range(GROUP):
                    row = turned(pieces[nj - 1], LANES - cols - SLOT * i)
                    row = jnp.where(lane < LANES - 4, turned(pieces[0], lon_count - SLOT * i), row)
                    for b in reversed(range(nj)):
                        row = jnp.where(lane < cols * (b + 1), turned(pieces[b], cols * b - SLOT * i), row)
                    field[k, tile((a * rows + h * GROUP + i + 2) * TILE), :] = row
        edges(field, k)

    def edges(padded, k):
        count = chunks[k][1]
        lines = lat_count * count // TILE
        for j in range(2):
            above, below = padded[k, tile((lines + j) * TILE), :], padded[k, tile((2 + j) * TILE), :]
            blank = jnp.zeros_like(above)
            if count < TILE:
                above = jnp.where(sublane >= count, pltpu.roll(above, count, 0), blank)
                below = jnp.where(sublane < TILE - count, pltpu.roll(below, TILE - count, 0), blank)
            else:
                above = below = blank
            padded[k, tile(j * TILE), :] = above
            padded[k, tile((lines + 2 + j) * TILE), :] = below

    def stencil(source, s, k, emit):
        step_rows = TILE
        for g in range(lat_count * chunks[k][1] // TILE // step_rows):
            base = g * step_rows
            lines = [source[k, tile((base + j) * TILE), :] for j in range(step_rows + 4)]
            sums = [lines[j + 2] for j in range(step_rows)]
            for b in range(5):
                weights = [taps[s, k, a * 5 + b] for a in range(5)]
                for j in range(step_rows):
                    term = weights[0] * lines[j]
                    for a in range(1, 5):
                        term = term + weights[a] * lines[j + a]
                    sums[j] = sums[j] + turned(term, 2 - b)
            emit(g, base, sums)

    def lines_of(k, c, skip):
        count = chunks[k][1]
        lines = lat_count * count // TILE
        return [pl.ds(skip * TILE + q * count + c, lines, stride=TILE) for q in range(TILE // count)]

    def transform(k):
        count = chunks[k][1]
        by_channel = jnp.concatenate(
            [first[k, at, :] for c in range(count) for at in lines_of(k, c, 0)], axis=0
        )
        high, low = halves(by_channel)
        coeffs = lax.dot_general(
            fwd[...], jnp.concatenate([high, low, high], axis=1), (((1,), (1,)), ((), ())),
            preferred_element_type=f32,
        )
        for p in range(count // 2):
            for r in range(2):
                part = [coeffs[(2 * s + r) * pairs : (2 * s + r + 1) * pairs, lanes_of(p)] for s in range(2)]
                even = jnp.where(low_half, part[0], pltpu.roll(part[1], HALF, 1))
                odd = jnp.where(low_half, pltpu.roll(part[0], HALF, 1), part[1])
                spec_in[k, pl.ds(r * TILE + 2 * p, pairs, stride=2 * TILE), :] = even
                spec_in[k, pl.ds(r * TILE + 2 * p + 1, pairs, stride=2 * TILE), :] = odd

    def lanes_of(p):
        return slice(p * LANES, (p + 1) * LANES)

    def degrees(k):
        gain = gain_col[pl.ds(start_of(k, la), TILE), :]
        gain = jnp.concatenate([gain, gain], axis=0)
        for m in range(pairs):
            at = pl.ds(m * 2 * TILE, 2 * TILE)
            spectrum = mm_wide(spec_in[k, at, :], into[m]) * gain
            spec_out[k, at, :] = mm_wide(spectrum, onto[m])

    def synthesis(k):
        count = chunks[k][1]
        rows_of = [[None] * (count // 2) for _ in range(4)]
        for p in range(count // 2):
            for r in range(2):
                even = spec_out[k, pl.ds(r * TILE + 2 * p, pairs, stride=2 * TILE), :]
                odd = spec_out[k, pl.ds(r * TILE + 2 * p + 1, pairs, stride=2 * TILE), :]
                rows_of[r][p] = jnp.where(low_half, even, pltpu.roll(odd, HALF, 1))
                rows_of[2 + r][p] = jnp.where(low_half, pltpu.roll(even, HALF, 1), odd)
        blank = jnp.zeros((LANES - 4 * pairs, LANES), f32)
        for p in range(count // 2):
            square = jnp.concatenate([rows_of[q][p] for q in range(4)] + [blank], axis=0).T
            high, low = halves(square)
            values = mm(jnp.concatenate([high, low, high], axis=1), back[...])
            for e in range(2):
                places = list(zip(lines_of(k, 2 * p + e, 0), lines_of(k, 2 * p + e, 2)))
                lines = lat_count // len(places)
                for q, (before, after) in enumerate(places):
                    base = e * lat_count + q * lines
                    second[k, after, :] = first[k, before, :] + values[base : base + lines]
        edges(second, k)

    def emit_first(k):
        def emit(g, base, sums):
            for j, row in enumerate(sums):
                first[k, tile((base + j) * TILE), :] = row
        return emit

    def emit_second(k):
        def emit(a, base, sums):
            for h in range(halves_count):
                for b in range(nj):
                    packed = None
                    for i in reversed(range(GROUP)):
                        moved = turned(sums[h * GROUP + i], SLOT * i - cols * b)
                        packed = moved if packed is None else jnp.where(lane < SLOT * (i + 1), moved, packed)
                    back_out[tile(((a * nj + b) * halves_count + h) * room + k * TILE), :] = packed
        return emit

    for k in range(len(chunks)):
        everyone(k, a_s, a_r).wait_recv()
        own_in(k).wait()
        if k + ahead < len(chunks):
            send_in(k + ahead)
        unpack(k)
        stencil(field, 0, k, emit_first(k))
        if k == 0:
            loads[4].wait()
        transform(k)
        if k == 0:
            loads[6].wait()
            loads[7].wait()
        degrees(k)
        if k == 0:
            loads[5].wait()
        synthesis(k)
        stencil(second, 1, k, emit_second(k))
        if whole_tile(k):
            for a in range(nl):
                band_tiles(k, a, fold, back_out)
        spread(k, z_copy)
        own_back(k).start()

    loads[3].wait()
    loads[8].wait()
    loads[9].wait()
    for k in range(len(chunks)):
        everyone(k, z_s, z_r).wait_recv()
        own_back(k).wait()
        if whole_tile(k):
            for h in range(halves_count):
                owner_tiles(k, h, unfold, home)
    for h in range(halves_count):
        for block in range(blocks):
            third[pl.ds(h * LANES, LANES), lanes(block)] = (
                home[h * channels + block * LANES : h * channels + (block + 1) * LANES, :].T
            )
    state = third[...]
    average = jnp.mean(state, axis=-1, keepdims=True)
    centred = state - average
    spread = jnp.mean(centred * centred, axis=-1, keepdims=True)
    normed = (centred * lax.rsqrt(spread + 1e-05) * norm_in[...].reshape(1, channels)).astype(bf16)
    active = jax.nn.gelu(mm(normed, up[...]), approximate=True).astype(bf16)
    result = state + mm(active, down[...])
    for block in range(blocks):
        for i in range(rows):
            grid[block, pl.ds(i, cols, stride=rows), :] = (
                result[SLOT * i : SLOT * i + cols, block * LANES : (block + 1) * LANES]
            )
        out[:, lanes(block)] = grid[block, 0 : rows * cols, :]
    for k in range(len(chunks)):
        everyone(k, a_s, a_r).wait_send()
        everyone(k, z_s, z_r).wait_send()


def fused(nl, nj, latent, conv_first, conv_second, filter_gains, norm_gain, up_weight, down_weight):
    rows, cols, channels = latent.shape
    modes, width = filter_gains.shape
    lat_count, lon_count = rows * nl, cols * nj
    forward, back, into, onto = (jnp.asarray(t) for t in constant_tables(lat_count, lon_count, modes))
    blocks = channels // LANES
    per = channels // (nl * nj)
    count = len(chunk_list(per))
    room = count * TILE
    halves_count = rows // GROUP
    vm = lambda *shape, kind=f32: pltpu.VMEM(shape, kind)
    dma = lambda *shape: pltpu.SemaphoreType.DMA(shape)
    far = pl.BlockSpec(memory_space=pltpu.HBM)
    result = pl.pallas_call(
        functools.partial(block_kernel, nl, nj, rows, modes),
        out_shape=pltpu.VMEM((cols * rows, channels), f32),
        in_specs=[far] * 11,
        out_specs=pl.BlockSpec(memory_space=pltpu.VMEM),
        scratch_shapes=[
            vm(blocks, rows * SLOT, LANES),
            vm(halves_count * channels, LANES),
            vm(nl * nj * halves_count * room, LANES),
            vm(count, (lat_count + 4) * TILE, LANES),
            vm(count, lat_count * TILE, LANES),
            vm(count, (lat_count + 4) * TILE, LANES),
            vm(count, modes * TILE, LANES),
            vm(count, modes * TILE, LANES),
            vm(nl * nj * halves_count * room, LANES),
            vm(halves_count * channels, LANES),
            vm(rows * SLOT, channels),
            vm(25, channels),
            vm(25, channels),
            vm(2, channels + TILE, 32),
            vm(2, count, 25, TILE, LANES),
            vm(modes, width),
            vm(LANES, width),
            vm(width + TILE, LANES),
            vm(channels),
            vm(*forward.shape, kind=bf16),
            vm(*back.shape, kind=bf16),
            vm(*into.shape, kind=bf16),
            vm(*onto.shape, kind=bf16),
            vm(*up_weight.shape, kind=bf16),
            vm(*down_weight.shape, kind=bf16),
            dma(10), dma(blocks), dma(count), dma(count),
            dma(count), dma(count), dma(count), dma(count),
        ],
        compiler_params=pltpu.CompilerParams(
            collective_id=0, has_side_effects=True, vmem_limit_bytes=60 * 1024 * 1024
        ),
        name="block",
    )(
        jnp.swapaxes(latent, 0, 1).reshape(cols * rows, channels), conv_first, conv_second,
        filter_gains, norm_gain, forward, back, into, onto, up_weight, down_weight,
    )
    return jnp.swapaxes(result.reshape(cols, rows, channels), 0, 1)


def fits(nl, nj, latent, filter_gains):
    rows, cols, channels = latent.shape
    modes = filter_gains.shape[0]
    total = nl * nj
    if rows != TILE or channels % LANES or channels % total or nj < 2 or nl < 2:
        return False
    if (channels // total) % GROUP or nl % 4 or rows * nl != HALF or cols > SLOT or cols != (TILE - 1) * (SLOT - cols) or (channels // (2 * channels // total)) % TILE or cols * nj > LANES - 8 or cols < 4:
        return False
    return modes % 16 == 0 and modes <= HALF and 2 * modes <= LANES


def body(latent, conv_first, conv_second, filter_gains, norm_gain, up_weight, down_weight):
    nl, nj = lax.axis_size("lat"), lax.axis_size("lon")
    arguments = (latent, conv_first, conv_second, filter_gains, norm_gain, up_weight, down_weight)
    if fits(nl, nj, latent, filter_gains):
        return fused(nl, nj, *arguments)
    return per_device(*arguments)


def solution(mesh):
    return jax.shard_map(
        body,
        mesh=mesh,
        in_specs=(P("lat", "lon", None), P(), P(), P(None, "lon"), P(), P(), P()),
        out_specs=P("lat", "lon", None),
        check_vma=False,
    )
```

```python
import functools
import math

import jax
import jax.numpy as jnp
import numpy as np
from jax import lax
from jax.experimental import pallas as pl
from jax.experimental.pallas import tpu as pltpu
from jax.sharding import PartitionSpec as P

highest = lax.Precision.HIGHEST


def padded_2(block, sides, width):
    for axis, dim in sides:
        count = lax.axis_size(axis)
        forward = [(i, i + 1) for i in range(count - 1)]
        backward = [(target, source) for source, target in forward]
        low = lax.ppermute(
            lax.slice_in_dim(block, block.shape[dim] - width, None, axis=dim), axis, forward
        )
        high = lax.ppermute(lax.slice_in_dim(block, 0, width, axis=dim), axis, backward)
        block = jnp.concatenate([low, block, high], axis=dim)
    return block


def stencil_sum(padded, weights, row_count, col_count):
    stencil_total = jnp.zeros((row_count, col_count, padded.shape[2]), padded.dtype)
    for row_shift in range(5):
        for col_shift in range(5):
            stencil_total = (
                stencil_total
                + weights[row_shift * 5 + col_shift]
                * padded[row_shift : row_shift + row_count, col_shift : col_shift + col_count, :]
            )
    return stencil_total


def slice_stencil(sliced, weights):
    lat_extended = padded_2(sliced, (("lat", 0),), 2)
    wrapped = jnp.concatenate([lat_extended[:, -2:], lat_extended, lat_extended[:, :2]], axis=1)
    return stencil_sum(wrapped, weights, sliced.shape[0], sliced.shape[1])


def colatitude(cell_count, float_type):
    cell_index = jnp.arange(cell_count).astype(float_type)
    return jnp.pi * (cell_index + 0.5) / cell_count


def legendre_table(orders, degrees, cosine, sine_theta):
    log_seed = 0.5 * (
        jnp.log((2.0 * orders + 1.0) / (4.0 * jnp.pi))
        + jax.scipy.special.gammaln(2.0 * orders + 1.0)
        - 2.0 * orders * jnp.log(2.0)
        - 2.0 * jax.scipy.special.gammaln(orders + 1.0)
    )
    diagonal_term = jnp.exp(log_seed[:, None] + orders[:, None] * jnp.log(sine_theta)[None, :])
    blanks = jnp.zeros_like(diagonal_term)
    legendre = jnp.zeros((orders.shape[0], degrees, sine_theta.shape[0]), diagonal_term.dtype)

    def block_step(block_index, state_tuple):
        previous, earlier, legendre = state_tuple
        values = []
        for offset in range(8):
            degree = (block_index * 8 + offset).astype(diagonal_term.dtype)
            square = degree * degree
            upper_ratio = jnp.sqrt(
                jnp.maximum(4.0 * square - 1.0, 1.0) / jnp.maximum(square - orders * orders, 1.0)
            )
            below_sq = (degree - 1.0) * (degree - 1.0)
            lower_ratio = jnp.sqrt(
                jnp.maximum(below_sq - orders * orders, 0.0)
                / jnp.maximum(4.0 * below_sq - 1.0, 1.0)
            )
            recurred = upper_ratio[:, None] * (
                cosine[None, :] * previous - lower_ratio[:, None] * earlier
            )
            current = jnp.where(
                (degree < orders)[:, None],
                blanks,
                jnp.where((degree == orders)[:, None], diagonal_term, recurred),
            )
            values.append(current)
            earlier = previous
            previous = current
        stacked = jnp.stack(values, axis=1)
        legendre = lax.dynamic_update_slice(
            legendre, stacked, (jnp.int32(0), (block_index * 8).astype(jnp.int32), jnp.int32(0))
        )
        return (previous, earlier, legendre)

    return lax.fori_loop(0, degrees // 8, block_step, (blanks, blanks, legendre))[2]


def fourier_tables(lon_count, mode_count, float_type):
    product_index = jnp.arange(lon_count)[:, None] * jnp.arange(mode_count)[None, :] % lon_count
    phase_grid = 2.0 * jnp.pi * product_index.astype(float_type) / lon_count
    forward = jnp.stack([jnp.cos(phase_grid), -jnp.sin(phase_grid)], axis=1) / lon_count
    factor = jnp.where(jnp.arange(mode_count) == 0, 1.0, 2.0).astype(float_type)
    inverse = jnp.stack(
        [jnp.cos(phase_grid).T * factor[:, None], -jnp.sin(phase_grid).T * factor[:, None]], axis=0
    )
    return (forward, inverse)


def channel_mlp(latent, norm_gain, up_weight, down_weight):
    average = jnp.mean(latent, axis=-1, keepdims=True)
    centred = latent - average
    spread = jnp.mean(centred * centred, axis=-1, keepdims=True)
    normed = (centred * lax.rsqrt(spread + 1e-05) * norm_gain).astype(jnp.bfloat16)
    hidden = jnp.dot(normed, up_weight, preferred_element_type=jnp.float32)
    active = jax.nn.gelu(hidden, approximate=True).astype(jnp.bfloat16)
    return latent + jnp.dot(active, down_weight, preferred_element_type=jnp.float32)


def per_device(latent, conv_first, conv_second, filter_gains, norm_gain, up_weight, down_weight):
    lat_size = lax.axis_size("lat")
    lon_size = lax.axis_size("lon")
    lat_local = latent.shape[0]
    lon_local = latent.shape[1]
    slice_width = filter_gains.shape[1]
    mode_count = filter_gains.shape[0]
    lat_count = lat_local * lat_size
    lon_count = lon_local * lon_size
    order_count = mode_count // lat_size
    channel_start = lax.axis_index("lon") * slice_width
    sliced = lax.all_to_all(latent, "lon", split_axis=2, concat_axis=1, tiled=True)
    first_taps = lax.dynamic_slice_in_dim(conv_first, channel_start, slice_width, 1)
    first_sliced = sliced + slice_stencil(sliced, first_taps)
    forward, inverse = fourier_tables(lon_count, mode_count, jnp.float32)
    colat_grid = colatitude(lat_count, jnp.float32)
    orders = (lax.axis_index("lat") * order_count + jnp.arange(order_count)).astype(jnp.float32)
    legendre = legendre_table(orders, mode_count, jnp.cos(colat_grid), jnp.sin(colat_grid))
    quadrature = 2.0 * jnp.pi * jnp.pi * jnp.sin(colat_grid) / lat_count
    weighted = legendre * quadrature
    coeffs = jnp.einsum("inc,nrk->irkc", first_sliced, forward, precision=highest)
    spectrum = jnp.einsum(
        "kli,irkc->lrkc",
        weighted,
        lax.all_to_all(coeffs, "lat", split_axis=2, concat_axis=0, tiled=True),
        precision=highest,
    )
    spectrum = spectrum * filter_gains[:, None, None, :]
    restored = jnp.einsum("kli,lrkc->irkc", legendre, spectrum, precision=highest)
    returned = lax.all_to_all(restored, "lat", split_axis=0, concat_axis=2, tiled=True)
    filtered = jnp.einsum("irkc,rkn->inc", returned, inverse, precision=highest)
    second_taps = lax.dynamic_slice_in_dim(conv_second, channel_start, slice_width, 1)
    second_sliced = first_sliced + filtered
    incoming = second_sliced + slice_stencil(second_sliced, second_taps)
    arrived = lax.all_to_all(incoming, "lon", split_axis=1, concat_axis=2, tiled=True)
    return channel_mlp(arrived, norm_gain, up_weight, down_weight)


LANES = 128
TILE = 8
GROUP = 4
SLOT = LANES // GROUP
HALF = LANES // 2
bf16 = jnp.bfloat16
f32 = jnp.float32


def legendre_numpy(modes, lat_count):
    theta = np.pi * (np.arange(lat_count) + 0.5) / lat_count
    cosine, sine = np.cos(theta), np.sin(theta)
    table = np.zeros((modes, modes, lat_count))
    for m in range(modes):
        seed = 0.5 * (
            math.log((2 * m + 1) / (4 * math.pi))
            + math.lgamma(2 * m + 1)
            - 2 * m * math.log(2.0)
            - 2 * math.lgamma(m + 1)
        )
        table[m, m] = np.exp(seed + m * np.log(sine))
        for l in range(m + 1, modes):
            a = math.sqrt((4.0 * l * l - 1) / (l * l - m * m))
            b = math.sqrt(max((l - 1.0) ** 2 - m * m, 0.0) / (4.0 * (l - 1.0) ** 2 - 1)) if l > 1 else 0.0
            earlier = table[m, l - 2] if l > m + 1 else 0.0
            table[m, l] = a * (cosine * table[m, l - 1] - b * earlier)
    quadrature = 2 * np.pi**2 * sine / lat_count
    return table, table * quadrature


def split_numpy(table):
    high = table.astype(np.float32).astype(jnp.bfloat16)
    low = (table - high.astype(np.float64)).astype(np.float32).astype(jnp.bfloat16)
    return high, low


@functools.lru_cache(maxsize=None)
def constant_tables(lat_count, lon_count, modes):
    pairs = modes // 2
    n = np.arange(lon_count)
    k = np.arange(modes)
    phase = 2 * np.pi * ((k[:, None] * n[None, :]) % lon_count) / lon_count
    trig = np.stack([np.cos(phase), -np.sin(phase)], axis=1)
    by_row = trig.reshape(2, pairs, 2, lon_count).transpose(0, 2, 1, 3).reshape(2 * modes, lon_count)
    forward = np.zeros((2 * modes, LANES))
    forward[:, :lon_count] = by_row / lon_count
    high, low = split_numpy(forward)
    forward = np.concatenate([high, high, low], axis=1)
    factor = np.where(k == 0, 1.0, 2.0)
    scaled = (trig * factor[:, None, None]).reshape(2, pairs, 2, lon_count).transpose(0, 2, 1, 3)
    scaled = scaled.reshape(2 * modes, lon_count)
    back = np.zeros((LANES, LANES))
    back[: 2 * modes, :lon_count] = scaled
    back[: 2 * modes, lon_count : lon_count + 2] = scaled[:, :2]
    back[: 2 * modes, LANES - 2 :] = scaled[:, lon_count - 2 :]
    high, low = split_numpy(back)
    back = np.concatenate([high, high, low], axis=0)
    table, weighted = legendre_numpy(modes, lat_count)
    into = np.zeros((pairs, LANES, LANES))
    onto = np.zeros((pairs, LANES, LANES))
    for s in range(2):
        part = slice(s * pairs, (s + 1) * pairs)
        lat, deg = slice(s * HALF, s * HALF + lat_count), slice(s * HALF, s * HALF + modes)
        into[:, lat, deg] = np.swapaxes(weighted[part], 1, 2)
        onto[:, deg, lat] = table[part]
    into = np.concatenate(split_numpy(into), axis=2)
    onto = np.concatenate(split_numpy(onto), axis=2)
    return forward, back, into, onto


def halves(value):
    high = value.astype(bf16)
    return high, (value - high.astype(f32)).astype(bf16)


def mm(a, b):
    return jnp.dot(a, b, preferred_element_type=f32)


def mm_wide(value, table):
    count = value.shape[0]
    high, low = halves(value)
    out = mm(jnp.concatenate([high, low], axis=0), table)
    return (out[:count, :LANES] + out[count:, :LANES]) + (out[:count, LANES:] + out[count:, LANES:])


def chunk_list(per):
    chunks = [(start, TILE) for start in range(0, per - per % TILE, TILE)]
    if per % TILE:
        chunks.append((per - per % TILE, per % TILE))
    return chunks[-1:] + chunks[:-1]


def block_kernel(
    nl, nj, rows, modes,
    latent, conv_first, conv_second, gains, norm_gain, fwd_hbm, back_hbm, into_hbm, onto_hbm, up_hbm, down_hbm,
    out,
    grid, sent, got, field, first, second, spec_in, spec_out, back_out, home, third,
    tap_one, tap_two, tap_col, taps, gain_in, gain_wide, gain_col, norm_in, fwd, back, into, onto, up, down,
    load_sem, in_sem, own_a, own_z, a_s, a_r, z_s, z_r,
):
    channels = latent.shape[1]
    cols = latent.shape[0] // rows
    blocks = channels // LANES
    total = nl * nj
    per = channels // total
    chunks = chunk_list(per)
    halves_count = rows // GROUP
    lat_count = rows * nl
    lon_count = cols * nj
    pairs = modes // 2
    la, lo = lax.axis_index("lat"), lax.axis_index("lon")
    me = lo * nl + la

    share = nl * per
    z_at, core = la // 2, lax.rem(la, 2)
    across = nl // 2

    def start_of(k, a):
        start, count = chunks[k]
        if per % TILE == 0:
            return a * per + start
        odd = lax.rem(a, 2)
        if count == TILE:
            return pl.multiple_of(a * per + odd * (per % TILE) + start, TILE)
        return a * per + (1 - odd) * start

    def rows_sent(k):
        return TILE - 1 if chunks[k][1] == TILE else chunks[k][1]

    def channels_of(k, a, b):
        return (slice(None), b, pl.ds(start_of(k, a), rows_sent(k)), slice(None))

    def place_of(k, a, b):
        count = chunks[k][1]
        bands = nl * count // TILE
        return (lax.rem(a, bands), b, slice(None), pl.ds(k * TILE + a // bands * count, rows_sent(k)), slice(None))

    def lanes(block):
        return pl.ds(block * LANES, LANES)

    def tile(start):
        return pl.ds(start if isinstance(start, int) else pl.multiple_of(start, TILE), TILE)

    def rcopy(src, dst, send, recv, a, b):
        return pltpu.make_async_remote_copy(
            src_ref=src, dst_ref=dst, send_sem=send, recv_sem=recv,
            device_id={"lat": a, "lon": b}, device_id_type=pl.DeviceIdType.MESH,
        )

    def others(action):
        for d in range(1, nj):
            action(la, lax.rem(lo + d, nj))

        def step(d, carry):
            a = lax.rem(la + d, nl)
            for b in range(nj):
                action(a, lax.rem(lo + b, nj))
            return carry

        lax.fori_loop(1, nl, step, 0)

    lane = lax.broadcasted_iota(jnp.int32, (TILE, LANES), 1)
    sublane = lax.broadcasted_iota(jnp.int32, (TILE, LANES), 0)
    within = lax.rem(lane, SLOT)
    wide = SLOT - cols
    room = len(chunks) * TILE
    by_owner = lambda ref: ref.reshape(halves_count, nj, share, LANES)
    by_band = lambda ref: ref.reshape(nl, nj, halves_count, room, LANES)

    def turned(row, shift):
        return pltpu.roll(row, shift % LANES, 1) if shift % LANES else row

    def fold(ref, start, stride):
        places = [pl.ds(start + c, TILE, stride=stride) for c in range(TILE)]
        lines = [ref[at, :] for at in places]
        for c in range(TILE - 1):
            ref[places[c], :] = jnp.where(within >= cols, turned(lines[-1], cols - wide * c), lines[c])

    def unfold(ref, start, stride):
        last = None
        for c in reversed(range(TILE - 1)):
            moved = turned(ref[pl.ds(start + c, TILE, stride=stride), :], wide * c - cols)
            last = moved if last is None else jnp.where(within < wide * (c + 1), moved, last)
        ref[pl.ds(start + TILE - 1, TILE, stride=stride), :] = last

    def owner_tiles(k, h, action, ref):
        odd = per % TILE
        step = 2 * per if odd else per
        for parity in range(step // per):
            base = h * channels + parity * (per + odd) + chunks[k][0]
            for group in range(channels // step // TILE):
                action(ref, base + group * TILE * step, step)

    def band_tiles(k, a, action, ref):
        action(ref, a * nj * halves_count * room + k * TILE, room)

    def whole_tile(k):
        return chunks[k][1] == TILE

    def in_copy(block):
        return pltpu.make_async_copy(
            latent.at[:, lanes(block)], grid.at[block, pl.ds(0, rows * cols)], in_sem.at[block]
        )

    for block in range(blocks):
        in_copy(block).start()

    barrier = pltpu.get_barrier_semaphore()
    others(
        lambda a, b: pl.semaphore_signal(
            barrier, inc=1, device_id={"lat": a, "lon": b}, device_id_type=pl.DeviceIdType.MESH
        )
    )

    pairs_of = (
        (conv_first, tap_one), (conv_second, tap_two), (gains, gain_in),
        (norm_gain, norm_in), (fwd_hbm, fwd), (back_hbm, back), (into_hbm, into), (onto_hbm, onto),
        (up_hbm, up), (down_hbm, down),
    )
    loads = [pltpu.make_async_copy(a, b, load_sem.at[i]) for i, (a, b) in enumerate(pairs_of)]


    for block in range(blocks):
        grid[block, rows * cols :, :] = jnp.zeros((rows * (SLOT - cols), LANES), f32)

    for block in range(blocks):
        in_copy(block).wait()
        if block + 1 == blocks:
            for load in loads:
                load.start()
        for h in range(halves_count):
            parts = [grid[block, pl.ds(h * GROUP + i, SLOT, stride=rows), :] for i in range(GROUP)]
            block_rows = jnp.concatenate(parts, axis=0).T
            sent[h * channels + block * LANES : h * channels + (block + 1) * LANES, :] = block_rows
    for k in range(len(chunks)):
        if whole_tile(k):
            for h in range(halves_count):
                owner_tiles(k, h, fold, sent)

    def a_copy(k, a, b):
        return rcopy(by_owner(sent).at[channels_of(k, a, b)], by_band(got).at[place_of(k, la, lo)], a_s.at[k], a_r.at[k], a, b)

    def z_copy(k, a, b):
        return rcopy(by_band(back_out).at[place_of(k, a, b)], by_owner(home).at[channels_of(k, la, lo)], z_s.at[k], z_r.at[k], a, b)

    def own_in(k):
        return pltpu.make_async_copy(by_owner(sent).at[channels_of(k, la, lo)], by_band(got).at[place_of(k, la, lo)], own_a.at[k])

    def own_back(k):
        return pltpu.make_async_copy(by_band(back_out).at[place_of(k, la, lo)], by_owner(home).at[channels_of(k, la, lo)], own_z.at[k])

    def everyone(k, send, recv):
        whole = first.at[0, pl.ds(0, (total - 1) * halves_count * rows_sent(k))]
        return rcopy(whole, whole, send.at[k], recv.at[k], lax.rem(la + 1, nl), lo)

    def spread(k, copy):
        def band(d, flip, start):
            a = lax.rem(z_at + d, across) * 2 + (1 - core if flip else core)
            for b in range(start, nj):
                copy(k, a, lax.rem(lo + b, nj)).start()

        for d in [1, across - 1, 0] + [e for q in range(2, across // 2 + 1) for e in sorted({q, across - q})]:
            band(d, False, 1 if d == 0 else 0)
            band(d, True, 0)

    pl.semaphore_wait(barrier, total - 1)
    def send_in(k):
        spread(k, a_copy)
        own_in(k).start()

    ahead = 2
    for k in range(ahead):
        send_in(k)

    loads[0].wait()
    loads[1].wait()
    loads[2].wait()
    gain_wide[...] = jnp.zeros_like(gain_wide)
    gain_wide[0:modes, :] = gain_in[...]
    gain_wide[HALF : HALF + modes, :] = gain_in[...]
    width = gain_in.shape[1]
    for start in range(0, width, LANES):
        stop = min(start + LANES, width)
        gain_col[start:stop, :] = gain_wide[:, start:stop].T
    for s, source in enumerate((tap_one, tap_two)):
        for block in range(blocks):
            square = jnp.concatenate([source[:, lanes(block)], jnp.zeros((7, LANES), f32)], axis=0)
            tap_col[s, lanes(block), :] = square.T
        for k, (_, count) in enumerate(chunks):
            own = tap_col[s, pl.ds(lo * share + start_of(k, la), TILE), :]
            if count < TILE:
                own = jnp.concatenate([own[:count]] * (TILE // count), axis=0)
            for t in range(25):
                taps[s, k, t] = jnp.broadcast_to(own[:, t : t + 1], (TILE, LANES))

    low_half = lax.broadcasted_iota(jnp.int32, (pairs, LANES), 1) < HALF

    def unpack(k):
        if whole_tile(k):
            for a in range(nl):
                band_tiles(k, a, unfold, got)
        for a in range(nl * chunks[k][1] // TILE):
            for h in range(halves_count):
                pieces = [got[tile(((a * nj + b) * halves_count + h) * room + k * TILE), :] for b in range(nj)]
                for i in range(GROUP):
                    row = turned(pieces[nj - 1], LANES - cols - SLOT * i)
                    row = jnp.where(lane < LANES - 4, turned(pieces[0], lon_count - SLOT * i), row)
                    for b in reversed(range(nj)):
                        row = jnp.where(lane < cols * (b + 1), turned(pieces[b], cols * b - SLOT * i), row)
                    field[k, tile((a * rows + h * GROUP + i + 2) * TILE), :] = row
        edges(field, k)

    def edges(padded, k):
        count = chunks[k][1]
        lines = lat_count * count // TILE
        for j in range(2):
            above, below = padded[k, tile((lines + j) * TILE), :], padded[k, tile((2 + j) * TILE), :]
            blank = jnp.zeros_like(above)
            if count < TILE:
                above = jnp.where(sublane >= count, pltpu.roll(above, count, 0), blank)
                below = jnp.where(sublane < TILE - count, pltpu.roll(below, TILE - count, 0), blank)
            else:
                above = below = blank
            padded[k, tile(j * TILE), :] = above
            padded[k, tile((lines + 2 + j) * TILE), :] = below

    def stencil(source, s, k, emit):
        step_rows = TILE
        for g in range(lat_count * chunks[k][1] // TILE // step_rows):
            base = g * step_rows
            lines = [source[k, tile((base + j) * TILE), :] for j in range(step_rows + 4)]
            sums = [lines[j + 2] for j in range(step_rows)]
            for b in range(5):
                weights = [taps[s, k, a * 5 + b] for a in range(5)]
                for j in range(step_rows):
                    term = weights[0] * lines[j]
                    for a in range(1, 5):
                        term = term + weights[a] * lines[j + a]
                    sums[j] = sums[j] + turned(term, 2 - b)
            emit(g, base, sums)

    def lines_of(k, c, skip):
        count = chunks[k][1]
        lines = lat_count * count // TILE
        return [pl.ds(skip * TILE + q * count + c, lines, stride=TILE) for q in range(TILE // count)]

    def transform(k):
        count = chunks[k][1]
        by_channel = jnp.concatenate(
            [first[k, at, :] for c in range(count) for at in lines_of(k, c, 0)], axis=0
        )
        high, low = halves(by_channel)
        coeffs = lax.dot_general(
            fwd[...], jnp.concatenate([high, low, high], axis=1), (((1,), (1,)), ((), ())),
            preferred_element_type=f32,
        )
        for p in range(count // 2):
            for r in range(2):
                part = [coeffs[(2 * s + r) * pairs : (2 * s + r + 1) * pairs, lanes_of(p)] for s in range(2)]
                even = jnp.where(low_half, part[0], pltpu.roll(part[1], HALF, 1))
                odd = jnp.where(low_half, pltpu.roll(part[0], HALF, 1), part[1])
                spec_in[k, pl.ds(r * TILE + 2 * p, pairs, stride=2 * TILE), :] = even
                spec_in[k, pl.ds(r * TILE + 2 * p + 1, pairs, stride=2 * TILE), :] = odd

    def lanes_of(p):
        return slice(p * LANES, (p + 1) * LANES)

    def degrees(k):
        gain = gain_col[pl.ds(start_of(k, la), TILE), :]
        gain = jnp.concatenate([gain, gain], axis=0)
        for m in range(pairs):
            at = pl.ds(m * 2 * TILE, 2 * TILE)
            spectrum = mm_wide(spec_in[k, at, :], into[m]) * gain
            spec_out[k, at, :] = mm_wide(spectrum, onto[m])

    def synthesis(k):
        count = chunks[k][1]
        rows_of = [[None] * (count // 2) for _ in range(4)]
        for p in range(count // 2):
            for r in range(2):
                even = spec_out[k, pl.ds(r * TILE + 2 * p, pairs, stride=2 * TILE), :]
                odd = spec_out[k, pl.ds(r * TILE + 2 * p + 1, pairs, stride=2 * TILE), :]
                rows_of[r][p] = jnp.where(low_half, even, pltpu.roll(odd, HALF, 1))
                rows_of[2 + r][p] = jnp.where(low_half, pltpu.roll(even, HALF, 1), odd)
        blank = jnp.zeros((LANES - 4 * pairs, LANES), f32)
        for p in range(count // 2):
            square = jnp.concatenate([rows_of[q][p] for q in range(4)] + [blank], axis=0).T
            high, low = halves(square)
            values = mm(jnp.concatenate([high, low, high], axis=1), back[...])
            for e in range(2):
                places = list(zip(lines_of(k, 2 * p + e, 0), lines_of(k, 2 * p + e, 2)))
                lines = lat_count // len(places)
                for q, (before, after) in enumerate(places):
                    base = e * lat_count + q * lines
                    second[k, after, :] = first[k, before, :] + values[base : base + lines]
        edges(second, k)

    def emit_first(k):
        def emit(g, base, sums):
            for j, row in enumerate(sums):
                first[k, tile((base + j) * TILE), :] = row
        return emit

    def emit_second(k):
        def emit(a, base, sums):
            for h in range(halves_count):
                for b in range(nj):
                    packed = None
                    for i in reversed(range(GROUP)):
                        moved = turned(sums[h * GROUP + i], SLOT * i - cols * b)
                        packed = moved if packed is None else jnp.where(lane < SLOT * (i + 1), moved, packed)
                    back_out[tile(((a * nj + b) * halves_count + h) * room + k * TILE), :] = packed
        return emit

    for k in range(len(chunks)):
        everyone(k, a_s, a_r).wait_recv()
        own_in(k).wait()
        if k + ahead < len(chunks):
            send_in(k + ahead)
        unpack(k)
        stencil(field, 0, k, emit_first(k))
        if k == 0:
            loads[4].wait()
        transform(k)
        if k == 0:
            loads[6].wait()
            loads[7].wait()
        degrees(k)
        if k == 0:
            loads[5].wait()
        synthesis(k)
        stencil(second, 1, k, emit_second(k))
        if whole_tile(k):
            for a in range(nl):
                band_tiles(k, a, fold, back_out)
        spread(k, z_copy)
        own_back(k).start()

    loads[3].wait()
    loads[8].wait()
    loads[9].wait()
    for k in range(len(chunks)):
        everyone(k, z_s, z_r).wait_recv()
        own_back(k).wait()
        if whole_tile(k):
            for h in range(halves_count):
                owner_tiles(k, h, unfold, home)
    for h in range(halves_count):
        for block in range(blocks):
            third[pl.ds(h * LANES, LANES), lanes(block)] = (
                home[h * channels + block * LANES : h * channels + (block + 1) * LANES, :].T
            )
    for h in range(halves_count):
        state = third[pl.ds(h * LANES, LANES), :]
        average = jnp.mean(state, axis=-1, keepdims=True)
        centred = state - average
        spread_of = jnp.mean(centred * centred, axis=-1, keepdims=True)
        normed = (centred * lax.rsqrt(spread_of + 1e-05) * norm_in[...].reshape(1, channels)).astype(bf16)
        active = jax.nn.gelu(mm(normed, up[...]), approximate=True).astype(bf16)
        result = state + mm(active, down[...])
        for block in range(blocks):
            for i in range(GROUP):
                grid[block, pl.ds(h * GROUP + i, cols, stride=rows), :] = (
                    result[SLOT * i : SLOT * i + cols, block * LANES : (block + 1) * LANES]
                )
    for block in range(blocks):
        out[:, lanes(block)] = grid[block, 0 : rows * cols, :]
    for k in range(len(chunks)):
        everyone(k, a_s, a_r).wait_send()
        everyone(k, z_s, z_r).wait_send()


def fused(nl, nj, latent, conv_first, conv_second, filter_gains, norm_gain, up_weight, down_weight):
    rows, cols, channels = latent.shape
    modes, width = filter_gains.shape
    lat_count, lon_count = rows * nl, cols * nj
    forward, back, into, onto = (jnp.asarray(t) for t in constant_tables(lat_count, lon_count, modes))
    blocks = channels // LANES
    per = channels // (nl * nj)
    count = len(chunk_list(per))
    room = count * TILE
    halves_count = rows // GROUP
    vm = lambda *shape, kind=f32: pltpu.VMEM(shape, kind)
    dma = lambda *shape: pltpu.SemaphoreType.DMA(shape)
    far = pl.BlockSpec(memory_space=pltpu.HBM)
    result = pl.pallas_call(
        functools.partial(block_kernel, nl, nj, rows, modes),
        out_shape=pltpu.VMEM((cols * rows, channels), f32),
        in_specs=[far] * 11,
        out_specs=pl.BlockSpec(memory_space=pltpu.VMEM),
        scratch_shapes=[
            vm(blocks, rows * SLOT, LANES),
            vm(halves_count * channels, LANES),
            vm(nl * nj * halves_count * room, LANES),
            vm(count, (lat_count + 4) * TILE, LANES),
            vm(count, lat_count * TILE, LANES),
            vm(count, (lat_count + 4) * TILE, LANES),
            vm(count, modes * TILE, LANES),
            vm(count, modes * TILE, LANES),
            vm(nl * nj * halves_count * room, LANES),
            vm(halves_count * channels, LANES),
            vm(rows * SLOT, channels),
            vm(25, channels),
            vm(25, channels),
            vm(2, channels + TILE, 32),
            vm(2, count, 25, TILE, LANES),
            vm(modes, width),
            vm(LANES, width),
            vm(width + TILE, LANES),
            vm(channels),
            vm(*forward.shape, kind=bf16),
            vm(*back.shape, kind=bf16),
            vm(*into.shape, kind=bf16),
            vm(*onto.shape, kind=bf16),
            vm(*up_weight.shape, kind=bf16),
            vm(*down_weight.shape, kind=bf16),
            dma(10), dma(blocks), dma(count), dma(count),
            dma(count), dma(count), dma(count), dma(count),
        ],
        compiler_params=pltpu.CompilerParams(
            collective_id=0, has_side_effects=True, vmem_limit_bytes=60 * 1024 * 1024
        ),
        name="block",
    )(
        jnp.swapaxes(latent, 0, 1).reshape(cols * rows, channels), conv_first, conv_second,
        filter_gains, norm_gain, forward, back, into, onto, up_weight, down_weight,
    )
    return jnp.swapaxes(result.reshape(cols, rows, channels), 0, 1)


def fits(nl, nj, latent, filter_gains):
    rows, cols, channels = latent.shape
    modes = filter_gains.shape[0]
    total = nl * nj
    if rows != TILE or channels % LANES or channels % total or nj < 2 or nl < 2:
        return False
    if (channels // total) % GROUP or nl % 4 or rows * nl != HALF or cols > SLOT or cols != (TILE - 1) * (SLOT - cols) or (channels // (2 * channels // total)) % TILE or cols * nj > LANES - 8 or cols < 4:
        return False
    return modes % 16 == 0 and modes <= HALF and 2 * modes <= LANES


def body(latent, conv_first, conv_second, filter_gains, norm_gain, up_weight, down_weight):
    nl, nj = lax.axis_size("lat"), lax.axis_size("lon")
    arguments = (latent, conv_first, conv_second, filter_gains, norm_gain, up_weight, down_weight)
    if fits(nl, nj, latent, filter_gains):
        return fused(nl, nj, *arguments)
    return per_device(*arguments)


def solution(mesh):
    return jax.shard_map(
        body,
        mesh=mesh,
        in_specs=(P("lat", "lon", None), P(), P(), P(None, "lon"), P(), P(), P()),
        out_specs=P("lat", "lon", None),
        check_vma=False,
    )
```
